32 devices in a mesh: groups: 2 (over y), gz: 4 (over x, core), xy: 4 (over z).
Axes of the slice: x: 2, y: 2, z: 4, core: 2. Of those that a mesh axis runs over, the one named last changes fastest.
Arguments:
- features: bfloat16 [16, 32, 32, 128], P(('groups', 'gz'), 'xy'), parts along dimension 0, may hold values from -6 to 6
- species: int32 [16, 32, 32], P(('groups', 'gz'), 'xy'), parts along dimension 0, may hold values from 0 to 7
- sublayer: int32 [16, 32, 32], P(('groups', 'gz'), 'xy'), parts along dimension 0, may hold values from 0 to 1
- offsets: float32 [2, 16, 32, 32], P(None, ('groups', 'gz'), 'xy'), parts along dimension 1, may hold values from 0 to 11
- neighbours: int32 [16, 32, 32, 32], P(('groups', 'gz'), 'xy'), parts along dimension 0, may hold values from 0 to 287
- neighbour_count: int32 [16, 32, 32], P(('groups', 'gz'), 'xy'), parts along dimension 0, may hold values from 16 to 32
- distances: float32 [16, 32, 32, 32], P(('groups', 'gz'), 'xy'), parts along dimension 0, may hold values from 0.8 to 7.8
- species_table: bfloat16 [8, 128], replicated, may hold values from -3 to 3
- charge_weight: bfloat16 [128, 16], replicated, may hold values from -0.5 to 0.5
- radial_in: bfloat16 [8, 64], replicated, may hold values from -2 to 2
- radial_out: bfloat16 [64, 128], replicated, may hold values from -0.75 to 0.75
- update_in: bfloat16 [128, 256], replicated, may hold values from -0.5 to 0.5
- update_out: bfloat16 [256, 128], replicated, may hold values from -0.375 to 0.375
- energy_weight: bfloat16 [128], replicated, may hold values from -0.5 to 0.5
Outputs:
- features_out: bfloat16 [16, 32, 32, 128], P(('groups', 'gz'), 'xy'), parts along dimension 0
- energy: float32 [16, 32, 32], P(('groups', 'gz'), 'xy'), parts along dimension 0
- forces: float32 [2, 16, 32, 32], P(None, ('groups', 'gz'), 'xy'), parts along dimension 1
The draws below stay inside these ranges and needn't reach their ends.
There are 2 independent parts, one for each index of `groups`. The reference program is written for one: setup_inputs(seed, part) draws one part's arguments, and reference() takes and returns one part's arrays. A program takes and returns all parts, laid end to end along the dimension named above; an argument that names none is the same for every part. Nothing has to cross between parts.
Inputs may be any that keep to these rules, and one draw needn't show every extreme that they name: `neighbours`: an entry n names the neighbour at cell offset o = n // 32 (z offset o // 3 - 1, x offset o % 3 - 1) and slot n % 32 of that cell. `neighbour_count`: entries of a list from this count on are padding.
All inputs are finite; a program needn't handle non-finite values.
Results may differ from the reference program's by a relative error of at most 0.0012.
The reference program's roundings to bfloat16 on the way count: a program that leaves them out, or rounds other values in their place, can miss the bound.
Values may be sent and summed in bfloat16 or wider, within the bound.
No kernel may reach another device: no remote copies, remote signals or barrier semaphores. Data moves between devices by JAX's collectives and lax.ppermute only.
A program may use at most 64 MiB of HBM per device.

```python
import math
import jax
import jax.numpy as jnp
from jax import lax

F = 128
C = 16
KX = 128
KY = 8
RH = 64
FH = 256
NRBF = 8
NSPEC = 8
NB = 32
SLOT = 32
NZ = 8
NX = 32


def with_ends(drawn, stream_key, least, largest):
    place = [jax.random.randint(jax.random.fold_in(stream_key, axis), (), 0, length) for axis, length in enumerate(drawn.shape)]
    main_axis = drawn.shape.index(max(drawn.shape))
    next_to = place[:main_axis] + [(place[main_axis] + 1) % drawn.shape[main_axis]] + place[main_axis + 1:]
    return drawn.at[tuple(place)].set(least).at[tuple(next_to)].set(largest)


def steps_of(rng, dims, shards, smallest, top_value):
    def one(dim, blocks):
        steps = jax.random.uniform(jax.random.fold_in(jax.random.fold_in(rng, 6), dim), (blocks,), jnp.float32, smallest / len(shards), top_value / len(shards))
        return jnp.repeat(jnp.exp(steps), dims[dim] // blocks).reshape((-1,) + (1,) * (len(dims) - dim - 1))

    level = one(*shards[0])
    for cut in shards[1:]:
        level = level * one(*cut)
    return level


def gaussian(key, shape, scale, most, split=(), kind=jnp.bfloat16):
    entries = jax.random.normal(key, shape, jnp.float32) * scale
    if len(split) > 0:
        entries = steps_of(key, shape, split, -0.22, 0.18) * entries
    return jnp.clip(entries, min=-most, max=most).astype(kind)


def setup_inputs(seed: int = 0, part: int = 0) -> dict:
    seeds = jax.random.split(jax.random.key(seed), 15)
    part_keys = jax.random.split(jax.random.fold_in(seeds[14], part), 15)
    features = gaussian(part_keys[0], (NZ, NX, SLOT, F), 1.0, 6.0, ((0, 4), (1, 4)))
    species = with_ends(jax.random.randint(part_keys[1], (NZ, NX, SLOT), 0, NSPEC), jax.random.fold_in(part_keys[1], 1), 0, NSPEC - 1).astype(jnp.int32)
    sublayer = with_ends(jax.random.randint(part_keys[2], (NZ, NX, SLOT), 0, 2), jax.random.fold_in(part_keys[2], 1), 0, 1).astype(jnp.int32)
    offsets = jnp.clip(11.0 * jax.random.uniform(part_keys[3], (2, NZ, NX, SLOT), jnp.float32) ** steps_of(part_keys[3], (2, NZ, NX, SLOT), ((1, 4), (2, 4)), -0.2, 0.2), 0.0, 11.0)
    neighbours = with_ends(jax.random.randint(part_keys[4], (NZ, NX, SLOT, NB), 0, 9 * SLOT), jax.random.fold_in(part_keys[4], 1), 0, (9 * SLOT) - 1).astype(jnp.int32)
    neighbour_count = with_ends(jax.random.randint(part_keys[5], (NZ, NX, SLOT), NB // 2, NB + 1), jax.random.fold_in(part_keys[5], 1), NB // 2, NB).astype(jnp.int32)
    distances = jnp.clip(0.8 + 7 * jax.random.uniform(part_keys[6], (NZ, NX, SLOT, NB), jnp.float32) ** steps_of(part_keys[6], (NZ, NX, SLOT, NB), ((0, 4), (1, 4)), -0.2, 0.2), 0.8, 7.8)
    species_table = gaussian(seeds[7], (NSPEC, F), 0.5, 3.0)
    charge_weight = gaussian(seeds[8], (F, C), F ** -0.5, 0.5)
    radial_in = gaussian(seeds[9], (NRBF, RH), NRBF ** -0.5, 2.0)
    radial_out = gaussian(seeds[10], (RH, F), RH ** -0.5, 0.75)
    update_in = gaussian(seeds[11], (F, FH), F ** -0.5, 0.5)
    update_out = gaussian(seeds[12], (FH, F), FH ** -0.5, 0.375)
    energy_weight = gaussian(seeds[13], (F,), F ** -0.5, 0.5)
    return dict(features=features, species=species, sublayer=sublayer, offsets=offsets, neighbours=neighbours, neighbour_count=neighbour_count, distances=distances, species_table=species_table, charge_weight=charge_weight, radial_in=radial_in, radial_out=radial_out, update_in=update_in, update_out=update_out, energy_weight=energy_weight)


cell_width = 11.0
layer_depth = 5.5
screening = 0.025
smearing = 1.0
coupling = 0.25
cutoff = 8.0
basis_width = 1.0

def wave_numbers(wave_index, width_x):
    wave_x = 2.0 * math.pi / width_x * (wave_index // KY - KX // 2).astype(jnp.float32)
    wave_y = 2.0 * math.pi / cell_width * (wave_index % KY - KY // 2).astype(jnp.float32)
    return (wave_x, wave_y)

def wave_factors(wave_x, wave_y, width_x):
    square = wave_x * wave_x + wave_y * wave_y
    screened = jnp.sqrt(square + screening * screening)
    weight = coupling * (2.0 * math.pi / (width_x * cell_width)) * jnp.exp(-0.5 * smearing * smearing * square) / screened
    return (screened, weight)

def build_panel(layer_field, wave_x, wave_y, weight):
    cosine = layer_field[:, :, 0] * weight
    sin_part = layer_field[:, :, 1] * weight
    cos_rows = jnp.stack([cosine, wave_x * sin_part, wave_y * sin_part], axis=1)
    sin_rows = jnp.stack([sin_part, -wave_x * cosine, -wave_y * cosine], axis=1)
    field_panel = jnp.stack([cos_rows, sin_rows], axis=3)
    shape = field_panel.shape
    return field_panel.reshape(shape[0], 3 * shape[2], 2, shape[4]).astype(jnp.bfloat16)

def phase_table(coord_x, coord_y, wave_x, wave_y):
    angles = coord_x[..., None] * wave_x + coord_y[..., None] * wave_y
    return jnp.concatenate([jnp.cos(angles), jnp.sin(angles)], axis=-1).astype(jnp.bfloat16)

def reference(features, species, sublayer, offsets, neighbours, neighbour_count, distances, species_table, charge_weight, radial_in, radial_out, update_in, update_out, energy_weight):
    z_count, x_count, slot_count, feature_width = features.shape
    channels = charge_weight.shape[1]
    wave_count = KX * KY
    width_x = cell_width * x_count
    hidden_start = (features.astype(jnp.float32) + species_table[species].astype(jnp.float32)).astype(jnp.bfloat16)
    charges = jnp.dot(hidden_start.reshape(-1, feature_width), charge_weight, preferred_element_type=jnp.float32)
    charges = charges.astype(jnp.bfloat16).reshape(z_count, x_count, slot_count, channels)
    wave_x, wave_y = wave_numbers(jnp.arange(wave_count, dtype=jnp.int32), width_x)
    screened, weight = wave_factors(wave_x, wave_y, width_x)
    decay = jnp.exp(-screened * layer_depth)
    cell_x = jnp.arange(x_count, dtype=jnp.int32).astype(jnp.float32)
    coord_x = cell_width * cell_x[None, :, None] + offsets[0]
    coord_y = offsets[1]

    def row_phases(z_row):
        return phase_table(coord_x[z_row].reshape(-1), coord_y[z_row].reshape(-1), wave_x, wave_y)

    def row_moments(z_row):
        phases = row_phases(z_row)
        layer_mask = (sublayer[z_row][..., None] == jnp.arange(2, dtype=jnp.int32)).astype(jnp.bfloat16)
        weighted = (layer_mask[..., :, None] * charges[z_row][..., None, :]).reshape(-1, 2 * channels)
        return jnp.dot(weighted.T, phases, preferred_element_type=jnp.float32)
    raw_moments = lax.map(row_moments, jnp.arange(z_count, dtype=jnp.int32))
    moments = raw_moments.reshape(2 * z_count, channels, 2, wave_count)

    def down_step(carried, layer_moments):
        renewed_sum = decay * carried + layer_moments
        return (renewed_sum, renewed_sum)

    def up_step(carried, layer_moments):
        return (decay * (carried + layer_moments), carried)
    start_carry = jnp.zeros((channels, 2, wave_count), jnp.float32)
    _, from_below = lax.scan(down_step, start_carry, moments)
    _, from_above = lax.scan(up_step, start_carry, moments, reverse=True)
    layer_field = from_below + from_above
    field_panel = build_panel(layer_field, wave_x, wave_y, weight).reshape(2 * z_count, 3 * channels, 2 * wave_count)
    z_padded = jnp.pad(hidden_start, ((1, 1), (0, 0), (0, 0), (0, 0)))
    padded = jnp.concatenate([z_padded[:, -1:], z_padded, z_padded[:, :1]], axis=1)
    own_slot = jnp.arange(slot_count, dtype=jnp.int32)[None, :, None]
    listed = jnp.arange(neighbours.shape[3], dtype=jnp.int32)
    cell_range = jnp.arange(x_count, dtype=jnp.int32)[:, None, None]
    basis_count = radial_in.shape[0]
    centers = cutoff * jnp.arange(basis_count, dtype=jnp.int32).astype(jnp.float32) / (basis_count - 1)

    def row_outputs(z_row):
        phases = row_phases(z_row)
        panel_pair = lax.dynamic_slice_in_dim(field_panel, 2 * z_row, 2, 0).reshape(6 * channels, 2 * wave_count)
        evaluated = lax.dot_general(phases, panel_pair, (((1,), (1,)), ((), ())), preferred_element_type=jnp.float32)
        evaluated = evaluated.reshape(x_count, slot_count, 2, 3, channels)
        chosen = jnp.where((sublayer[z_row] == 0)[..., None, None], evaluated[:, :, 0], evaluated[:, :, 1])
        charge_values = charges[z_row].astype(jnp.float32)
        long_energy = 0.5 * lax.optimization_barrier(jnp.sum(charge_values * chosen[:, :, 0], axis=-1))
        force_x = -lax.optimization_barrier(jnp.sum(charge_values * chosen[:, :, 1], axis=-1))
        force_y = -lax.optimization_barrier(jnp.sum(charge_values * chosen[:, :, 2], axis=-1))
        region = lax.dynamic_slice_in_dim(padded, z_row, 3, 0).reshape(-1, feature_width)
        codes = neighbours[z_row]
        offset_code = codes // slot_count
        slot_code = codes % slot_count
        row_index = (offset_code // 3 * (x_count + 2) + cell_range + offset_code % 3) * slot_count + slot_code
        gathered = jnp.take(region, row_index.reshape(-1), axis=0).reshape(x_count, slot_count, -1, feature_width)
        usable = (listed < neighbour_count[z_row][..., None]) & jnp.logical_not((offset_code == 4) & (slot_code == own_slot))
        spacing = distances[z_row]
        radial_basis = jnp.exp(-jnp.square((spacing[..., None] - centers) / basis_width)).astype(jnp.bfloat16)
        filter_hidden = jax.nn.silu(jnp.dot(radial_basis.reshape(-1, basis_count), radial_in, preferred_element_type=jnp.float32)).astype(jnp.bfloat16)
        filters = jnp.dot(filter_hidden, radial_out, preferred_element_type=jnp.float32).reshape(gathered.shape)
        envelope = jnp.square(1.0 - jnp.square(spacing / cutoff))
        edge_weight = jnp.where(usable, envelope, 0.0)
        aggregate = lax.optimization_barrier(jnp.sum(edge_weight[..., None] * filters * gathered.astype(jnp.float32), axis=2)).astype(jnp.bfloat16)
        update_hidden = jax.nn.silu(jnp.dot(aggregate.reshape(-1, feature_width), update_in, preferred_element_type=jnp.float32)).astype(jnp.bfloat16)
        renewed = hidden_start[z_row].astype(jnp.float32) + jnp.dot(update_hidden, update_out, preferred_element_type=jnp.float32).reshape(x_count, slot_count, feature_width)
        energy_row = lax.optimization_barrier(jnp.sum(renewed * energy_weight.astype(jnp.float32), axis=-1)) + long_energy
        return (renewed.astype(jnp.bfloat16), energy_row, jnp.stack([force_x, force_y]))
    features_out, energy, force_rows = lax.map(row_outputs, jnp.arange(z_count, dtype=jnp.int32))
    forces = jnp.moveaxis(force_rows, 1, 0)
    return (features_out, energy, forces)
```

```python
import math

import jax
import jax.numpy as jnp
from jax import lax
from jax.experimental import pallas as pl
from jax.experimental.pallas import tpu as pltpu
from jax.sharding import PartitionSpec as P

KX = 128
KY = 8

cell_width = 11.0
layer_depth = 5.5
screening = 0.025
smearing = 1.0
coupling = 0.25
cutoff = 8.0
basis_width = 1.0

HALF_X = KX // 2
HALF_Y = KY // 2
WAVES = 640

f32 = jnp.float32
bf16 = jnp.bfloat16

SIN_TERMS = (9.99999996e-01, -1.66666580e-01, 8.33305062e-03, -1.98090464e-04, 2.60516628e-06)
COS_TERMS = (9.99999953e-01, -4.99999051e-01, 4.16635789e-02, -1.38536669e-03, 2.31531742e-05)


def nt_dot(a, b):
    return lax.dot_general(a, b, (((1,), (1,)), ((), ())), preferred_element_type=f32)


def nn_dot(a, b):
    return lax.dot_general(a, b, (((1,), (0,)), ((), ())), preferred_element_type=f32)


def tn_dot(a, b):
    return lax.dot_general(a, b, (((0,), (0,)), ((), ())), preferred_element_type=f32)


def polynomial(z, terms):
    value = jnp.full_like(z, terms[-1])
    for term in terms[-2::-1]:
        value = value * z + term
    return value


def cos_sin(angle):
    turns = jnp.floor(angle * (1.0 / (2.0 * math.pi)) + 0.5)
    head = 6.28125
    rest = (angle - turns * head) - turns * (2.0 * math.pi - head)
    half = rest * 0.5
    z = half * half
    s = half * polynomial(z, SIN_TERMS)
    c = polynomial(z, COS_TERMS)
    return 1.0 - 2.0 * (s * s), 2.0 * (s * c)


def wave_row(width_x):
    lane = lax.broadcasted_iota(jnp.int32, (1, WAVES), 1)
    block = lane // HALF_X
    place = lane % HALF_X
    edge = block == 2 * HALF_Y + 1
    minus = (block > 0) & (block % 2 == 0)
    step_x = jnp.where(
        edge, jnp.where(place <= HALF_Y, HALF_X, -HALF_X), jnp.where(minus, -place, place)
    )
    step_y = jnp.where(
        edge, jnp.where(place <= HALF_Y, place, place - HALF_Y), (block + 1) // 2
    )
    inner = (place > 0) | ((block > 0) & (step_y < HALF_Y))
    twice = inner & ((step_y < HALF_Y))
    plain = jnp.where(minus & (place == 0), 0, jnp.where(twice, 2, 1))
    count = jnp.where(edge, jnp.where(place < 2 * HALF_Y, 1, 0), plain).astype(f32)
    wave_x = 2.0 * math.pi / width_x * step_x.astype(f32)
    wave_y = 2.0 * math.pi / cell_width * step_y.astype(f32)
    square = wave_x * wave_x + wave_y * wave_y
    screened = jnp.sqrt(square + screening * screening)
    weight = (
        coupling
        * (2.0 * math.pi / (width_x * cell_width))
        * jnp.exp(-0.5 * smearing * smearing * square)
        / screened
    )
    return wave_x, wave_y, screened, weight * count


def twin(row):
    return jnp.concatenate([row, row], axis=1)


def store_phases(out_ref, lanes, coord_x, coord_y, width_x):
    count = coord_x.shape[1]
    step_x = lax.broadcasted_iota(jnp.int32, (HALF_X + 8, count), 0).astype(f32)
    cos_x, sin_x = cos_sin((2.0 * math.pi / width_x * step_x) * coord_x)
    row = lax.broadcasted_iota(jnp.int32, (2 * HALF_Y, count), 0)
    step_y = jnp.where(row <= HALF_Y, row, row - HALF_Y).astype(f32)
    cos_y, sin_y = cos_sin((2.0 * math.pi / cell_width * step_y) * coord_y)
    main_c, main_s = cos_x[:HALF_X], sin_x[:HALF_X]

    def put(block, cosine, sine):
        rows = cosine.shape[0]
        out_ref[block * HALF_X : block * HALF_X + rows, lanes] = cosine.astype(bf16)
        out_ref[WAVES + block * HALF_X : WAVES + block * HALF_X + rows, lanes] = sine.astype(bf16)

    put(0, main_c, main_s)
    for b in range(1, HALF_Y + 1):
        cb, sb = cos_y[b : b + 1], sin_y[b : b + 1]
        cc, ss, sc, cs = main_c * cb, main_s * sb, main_s * cb, main_c * sb
        put(2 * b - 1, cc - ss, sc + cs)
        put(2 * b, cc + ss, cs - sc)
    edge_c = cos_x[HALF_X : HALF_X + 1]
    edge_s = jnp.where(row <= HALF_Y, sin_x[HALF_X : HALF_X + 1], -sin_x[HALF_X : HALF_X + 1])
    blank = jnp.zeros((HALF_X - 2 * HALF_Y, count), f32)
    put(
        2 * HALF_Y + 1,
        jnp.concatenate([edge_c * cos_y - edge_s * sin_y, blank], axis=0),
        jnp.concatenate([edge_s * cos_y + edge_c * sin_y, blank], axis=0),
    )


def layer_charges(charges, sub):
    return jnp.concatenate(
        [
            jnp.where(sub == 0.0, charges, 0.0).astype(bf16),
            jnp.where(sub == 1.0, charges, 0.0).astype(bf16),
        ],
        axis=0,
    )


def lane_rows(read, cells, slots):
    per = 128 // slots
    cat = jnp.concatenate(
        [read(pl.ds(j, cells // per, stride=per)) for j in range(per)], axis=1
    )
    return jnp.concatenate([cat[q : q + 1] for q in range(cells // per)], axis=1)


def three_parts(value):
    head = value.astype(bf16).astype(f32)
    middle = (value - head).astype(bf16).astype(f32)
    return [head, middle, (value - head) - middle]


def start_kernel(zcells, xcells, slots, place_ref, feat_ref, spec_ref, sub_ref, off_ref, table_ref,
                 cw_ref, hid_ref, msg_ref, right_ref, left_ref):
    cells = zcells * xcells
    atoms = cells * slots
    kinds = table_ref.shape[0]
    spec = lane_rows(lambda rows: spec_ref[rows, :], cells, slots)
    onehot = (lax.broadcasted_iota(jnp.int32, (kinds, atoms), 0) == spec).astype(f32)
    embedded = tn_dot(onehot, table_ref[...].astype(f32))
    hidden = (feat_ref[...].astype(f32) + embedded).astype(bf16)
    hid_ref[...] = hidden
    weight_t = cw_ref[...].astype(f32).T.astype(bf16)
    charges = nt_dot(weight_t, hidden).astype(bf16)
    channels = charges.shape[0]
    sub = lane_rows(lambda rows: sub_ref[rows, :], cells, slots).astype(f32)
    lane_cell = lax.broadcasted_iota(jnp.int32, (1, atoms), 1) // slots % xcells
    cell_x = (place_ref[0] * xcells + lane_cell).astype(f32)
    coord_x = cell_width * cell_x + lane_rows(lambda rows: off_ref[0, rows, :], cells, slots)
    coord_y = lane_rows(lambda rows: off_ref[1, rows, :], cells, slots)
    extra = jnp.concatenate(
        three_parts(coord_x)
        + three_parts(coord_y)
        + [sub, jnp.zeros((16 - 7, atoms), f32)],
        axis=0,
    ).astype(bf16)
    msg_ref[0:channels, :] = charges
    msg_ref[channels : channels + 16, :] = extra
    for ref, column in ((right_ref, xcells - 1), (left_ref, 0)):
        ref[0:channels, :] = charges
        ref[channels : channels + 16, :] = extra
        for z in range(zcells):
            for h in range(slots // 16):
                begin = (z * xcells + column) * slots + 16 * h
                lane = (z * (slots // 16) + h) * 128
                ref[channels + 16 : channels + 32, lane : lane + 128] = hid_ref[
                    begin : begin + 16, :
                ]


def read_atoms(msg_ref, channels, lanes):
    charges = msg_ref[0:channels, lanes].astype(f32)
    extra = msg_ref[channels : channels + 16, lanes].astype(f32)
    coord_x = (extra[0:1] + extra[1:2]) + extra[2:3]
    coord_y = (extra[3:4] + extra[4:5]) + extra[5:6]
    return charges, coord_x, coord_y, extra[6:7]


def own_kernel(zcells, channels, width_x, msg_ref, phase_ref, moment_ref):
    row_atoms = msg_ref.shape[1] // zcells
    for z in range(zcells):
        lanes = slice(z * row_atoms, (z + 1) * row_atoms)
        charges, coord_x, coord_y, sub = read_atoms(msg_ref, channels, lanes)
        store_phases(phase_ref, lanes, coord_x, coord_y, width_x)
        moment_ref[z] = nt_dot(layer_charges(charges, sub), phase_ref[:, lanes])


def slab_kernel(zcells, channels, width_x, slabs, others, place_ref, own_ref, *refs):
    msg_refs = refs[:others]
    moment_ref = refs[others]
    send_refs = refs[others + 1 : others + slabs]
    scratch = refs[others + slabs]
    row_atoms = msg_refs[0].shape[1] // zcells
    for z in range(zcells):
        total = own_ref[z]
        for ref in msg_refs:
            lanes = slice(z * row_atoms, (z + 1) * row_atoms)
            charges, coord_x, coord_y, sub = read_atoms(ref, channels, lanes)
            store_phases(scratch, slice(0, row_atoms), coord_x, coord_y, width_x)
            total = total + nt_dot(layer_charges(charges, sub), scratch[...])
        moment_ref[z] = total
    screened = wave_row(width_x)[2]
    decay = twin(jnp.exp(-screened * layer_depth))
    layers = [
        moment_ref[z, l * channels : (l + 1) * channels, :] for z in range(zcells) for l in range(2)
    ]
    top = layers[0]
    for layer in layers[1:]:
        top = decay * top + layer
    bottom = decay * layers[-1]
    for layer in layers[-2::-1]:
        bottom = decay * (bottom + layer)
    for shift, ref in enumerate(send_refs, start=1):
        ref[...] = jnp.where(place_ref[1] + shift < slabs, top, bottom)


def edge_kernel(zcells, xcells, slots, channels, hid_ref, below_ref, above_ref, left_ref,
                right_ref, near_ref, dist_ref, count_ref, rin_ref, rout_ref, uin_ref, uout_ref,
                ew_ref, out_ref, energy_ref, ext_ref):
    features = hid_ref.shape[1]
    wide = (xcells + 2) * slots
    listed = near_ref.shape[2]
    ext_ref[0] = below_ref[...]
    ext_ref[zcells + 1] = above_ref[...]
    for z in range(zcells):
        ext_ref[z + 1, slots : slots + xcells * slots, :] = hid_ref[
            z * xcells * slots : (z + 1) * xcells * slots, :
        ]
        for h in range(slots // 16):
            lane = (z * (slots // 16) + h) * 128
            ext_ref[z + 1, 16 * h : 16 * h + 16, :] = left_ref[
                channels + 16 : channels + 32, lane : lane + 128
            ]
            ext_ref[z + 1, wide - slots + 16 * h : wide - slots + 16 * h + 16, :] = right_ref[
                channels + 16 : channels + 32, lane : lane + 128
            ]
    rin_t = rin_ref[...].astype(f32).T.astype(bf16)
    rout_t = rout_ref[...].astype(f32).T.astype(bf16)
    uin_t = uin_ref[...].astype(f32).T.astype(bf16)
    basis = rin_ref.shape[0]
    lane_groups = 128 // slots
    chunk_rows = listed // lane_groups
    region = 9 * slots // 2
    centre = (
        cutoff * lax.broadcasted_iota(jnp.int32, (basis, 256), 0).astype(f32) / (basis - 1)
    )
    row_id = lax.broadcasted_iota(jnp.int32, (region, 256), 0)
    lane8 = lax.broadcasted_iota(jnp.int32, (chunk_rows, 128), 1)
    sub8 = lax.broadcasted_iota(jnp.int32, (chunk_rows, 128), 0)
    slot8 = lane8 % slots
    listed8 = (lane8 // slots) * chunk_rows + sub8
    group_lane = lax.broadcasted_iota(jnp.int32, (features, 128), 1) // slots

    def edge_rows(block):
        turned = block.T
        return jnp.concatenate(
            [turned[g * chunk_rows : (g + 1) * chunk_rows] for g in range(lane_groups)], axis=1
        )

    def one_cell(cell):
        z = cell // xcells
        x = cell % xcells
        begin = pl.multiple_of(x * slots, slots)
        rows = jnp.concatenate(
            [ext_ref[z + dz, pl.ds(begin, 3 * slots), :] for dz in range(3)], axis=0
        )
        rows_t = jnp.concatenate(
            [rows[:region].astype(f32).T, rows[region:].astype(f32).T], axis=0
        ).astype(bf16)
        near = edge_rows(near_ref[cell].astype(f32)).astype(jnp.int32)
        dist = edge_rows(dist_ref[cell])
        count = count_ref[pl.ds(cell, 1), :]
        count = jnp.concatenate([count] * lane_groups, axis=1)
        itself = near == 4 * slots + slot8
        usable = (listed8 < count) & jnp.logical_not(itself)
        part = 1.0 - jnp.square(dist * (1.0 / cutoff))
        weight = jnp.where(usable, part * part, 0.0)
        upper = jnp.where(near >= region, 1.0, 0.0)
        index = jnp.where(near >= region, near - region, near)
        total = jnp.zeros((features, 128), f32)
        for q in range(0, chunk_rows, 2):
            def pair(table):
                return jnp.concatenate([table[q : q + 1], table[q + 1 : q + 2]], axis=1)

            onehot = jnp.where(row_id == pair(index), 1.0, 0.0).astype(bf16)
            both = nn_dot(rows_t, onehot)
            gap = (pair(dist) - centre) / basis_width
            radial = jnp.exp(-(gap * gap)).astype(bf16)
            half = 0.5 * nn_dot(rin_t, radial)
            hidden = (half + half * jnp.tanh(half)).astype(bf16)
            filters = nn_dot(rout_t, hidden)
            picked = jnp.where(pair(upper) > 0.5, both[features:], both[:features])
            product = (pair(weight) * filters) * picked
            total = total + (product[:, :128] + product[:, 128:])
        shift = 64
        while shift >= slots:
            total = total + pltpu.roll(total, shift, 1)
            shift //= 2
        return total

    def four_cells(step, carry):
        merged = one_cell(step * lane_groups)
        for g in range(1, lane_groups):
            merged = jnp.where(group_lane == g, one_cell(step * lane_groups + g), merged)
        aggregate = merged.astype(bf16)
        half = 0.5 * nn_dot(uin_t, aggregate)
        hidden = (half + half * jnp.tanh(half)).astype(bf16)
        begin = pl.multiple_of(step * 128, 128)
        renewed = hid_ref[pl.ds(begin, 128), :].astype(f32) + nn_dot(
            hidden.astype(f32).T.astype(bf16), uout_ref[...]
        )
        out_ref[pl.ds(begin, 128), :] = renewed.astype(bf16)
        weighted = renewed * ew_ref[...].astype(f32)
        energy_ref[pl.ds(step, 1), :] = jnp.sum(weighted.T, axis=0, keepdims=True)
        return carry

    lax.fori_loop(0, zcells * xcells // lane_groups, four_cells, 0)


def field_kernel(zcells, xcells, slots, channels, width_x, slabs, place_ref, msg_ref, phase_ref,
                 moment_ref, short_ref, *refs):
    sums = refs[: slabs - 1]
    energy_ref, force_ref = refs[slabs - 1 :]
    wave_x, wave_y, screened, weight = wave_row(width_x)
    decay = twin(jnp.exp(-screened * layer_depth))
    span = decay
    for _ in range(2 * zcells - 1):
        span = span * decay
    place = place_ref[1]
    below = jnp.zeros_like(sums[0][...])
    above = jnp.zeros_like(below)
    for shift in range(slabs - 1, 0, -1):
        below = jnp.where(place >= shift, below * span + sums[shift - 1][...], below)
    for shift in range(1, slabs):
        above = jnp.where(place < shift, above * span + sums[shift - 1][...], above)
    layers = [
        moment_ref[z, l * channels : (l + 1) * channels, :] for z in range(zcells) for l in range(2)
    ]
    down = []
    for layer in layers:
        below = decay * below + layer
        down.append(below)
    up = [above]
    for layer in layers[:0:-1]:
        above = decay * (above + layer)
        up.append(above)
    up = up[::-1]
    row_atoms = xcells * slots
    for z in range(zcells):
        lanes = slice(z * row_atoms, (z + 1) * row_atoms)
        rows = []
        for l in range(2):
            field = down[2 * z + l] + up[2 * z + l]
            cosine = field[:, :WAVES] * weight
            sine = field[:, WAVES:] * weight
            rows.append(jnp.concatenate([cosine, sine], axis=1))
            rows.append(jnp.concatenate([wave_x * sine, -wave_x * cosine], axis=1))
            rows.append(jnp.concatenate([wave_y * sine, -wave_y * cosine], axis=1))
        panel = jnp.concatenate([row.astype(bf16) for row in rows], axis=0)
        evaluated = nn_dot(panel, phase_ref[:, lanes])
        sub = msg_ref[channels : channels + 16, lanes].astype(f32)[6:7]
        chosen = jnp.where(sub == 0.0, evaluated[: 3 * channels], evaluated[3 * channels :])
        charges = msg_ref[0:channels, lanes].astype(f32)
        long_energy = 0.5 * jnp.sum(charges * chosen[:channels], axis=0, keepdims=True)
        force_x = -jnp.sum(charges * chosen[channels : 2 * channels], axis=0, keepdims=True)
        force_y = -jnp.sum(charges * chosen[2 * channels :], axis=0, keepdims=True)
        per = row_atoms // 128
        short = jnp.concatenate(
            [short_ref[z * per + j : z * per + j + 1, :] for j in range(per)], axis=1
        )
        energy = short + long_energy
        for x in range(xcells):
            cell = z * xcells + x
            piece = slice(x * slots, (x + 1) * slots)
            energy_ref[cell : cell + 1, :] = energy[:, piece]
            force_ref[0, cell : cell + 1, :] = force_x[:, piece]
            force_ref[1, cell : cell + 1, :] = force_y[:, piece]


def vmem():
    return pl.BlockSpec(memory_space=pltpu.VMEM)


def smem():
    return pl.BlockSpec(memory_space=pltpu.SMEM)


def shards(
    features,
    species,
    sublayer,
    offsets,
    neighbours,
    neighbour_count,
    distances,
    species_table,
    charge_weight,
    radial_in,
    radial_out,
    update_in,
    update_out,
    energy_weight,
):
    zcells, xcells, slots, width = features.shape
    channels = charge_weight.shape[1]
    listed = neighbours.shape[3]
    cells = zcells * xcells
    atoms = cells * slots
    strips = lax.axis_size("xy")
    slabs = lax.axis_size("gz")
    width_x = cell_width * (xcells * strips)
    place = jnp.stack([lax.axis_index("xy"), lax.axis_index("gz")]).astype(jnp.int32)

    def shape(dims, kind):
        return jax.ShapeDtypeStruct(dims, kind)

    def partial(body, *static):
        def kernel(*refs):
            body(*static, *refs)

        kernel.__name__ = body.__name__
        return kernel

    def cost(flops, data):
        return pl.CostEstimate(flops=flops, bytes_accessed=data, transcendentals=0)

    hidden, message, to_right, to_left = pl.pallas_call(
        partial(start_kernel, zcells, xcells, slots),
        out_shape=(
            shape((atoms, width), bf16),
            shape((channels + 16, atoms), bf16),
            shape((channels + 32, atoms), bf16),
            shape((channels + 32, atoms), bf16),
        ),
        in_specs=[smem()] + [vmem()] * 6,
        out_specs=(vmem(),) * 4,
    )(
        place,
        features.reshape(atoms, width),
        species.reshape(cells, slots),
        sublayer.reshape(cells, slots),
        offsets.reshape(2, cells, slots),
        species_table,
        charge_weight,
    )

    def ring(count, shift):
        return [(i, (i + shift) % count) for i in range(count)]

    from_left = lax.ppermute(to_right, "xy", ring(strips, 1))
    from_right = lax.ppermute(to_left, "xy", ring(strips, strips - 1))
    messages = [from_left, from_right] + [
        lax.ppermute(message, "xy", ring(strips, shift)) for shift in range(2, strips - 1)
    ]

    phases, own_moments = pl.pallas_call(
        partial(own_kernel, zcells, channels, width_x),
        out_shape=(
            shape((2 * WAVES, atoms), bf16),
            shape((zcells, 2 * channels, 2 * WAVES), f32),
        ),
        in_specs=[vmem()],
        out_specs=(vmem(), vmem()),
        cost_estimate=cost(4_000_000_000, 2_000_000),
    )(message)

    slab = pl.pallas_call(
        partial(slab_kernel, zcells, channels, width_x, slabs, len(messages)),
        out_shape=(shape((zcells, 2 * channels, 2 * WAVES), f32),)
        + (shape((channels, 2 * WAVES), f32),) * (slabs - 1),
        in_specs=[smem()] + [vmem()] * (1 + len(messages)),
        out_specs=(vmem(),) * slabs,
        scratch_shapes=[pltpu.VMEM((2 * WAVES, atoms // zcells), bf16)],
        cost_estimate=cost(8_000_000_000, 2_000_000),
    )(place, own_moments, *messages)
    moments = slab[0]

    def column(received, z):
        rows = received[channels + 16 :].reshape(16, -1, width)
        first = z * (slots // 16)
        return jnp.concatenate([rows[:, first + h] for h in range(slots // 16)], axis=0)

    row_atoms = xcells * slots

    def extended(z):
        return jnp.concatenate(
            [
                column(from_left, z),
                hidden[z * row_atoms : (z + 1) * row_atoms],
                column(from_right, z),
            ],
            axis=0,
        )

    below = lax.ppermute(extended(zcells - 1), "gz", [(i, i + 1) for i in range(slabs - 1)])
    above = lax.ppermute(extended(0), "gz", [(i + 1, i) for i in range(slabs - 1)])
    sums = [
        lax.ppermute(slab[shift], "gz", ring(slabs, shift)) for shift in range(1, slabs)
    ]

    features_out, short_energy = pl.pallas_call(
        partial(edge_kernel, zcells, xcells, slots, channels),
        out_shape=(shape((atoms, width), bf16), shape((atoms // 128, 128), f32)),
        in_specs=[vmem()] * 13,
        out_specs=(vmem(), vmem()),
        scratch_shapes=[pltpu.VMEM((zcells + 2, (xcells + 2) * slots, width), bf16)],
        cost_estimate=cost(12_000_000_000, 4_000_000),
    )(
        hidden,
        below,
        above,
        from_left,
        from_right,
        neighbours.reshape(cells, slots, listed),
        distances.reshape(cells, slots, listed),
        neighbour_count.reshape(cells, slots),
        radial_in,
        radial_out,
        update_in,
        update_out,
        energy_weight.reshape(1, width),
    )

    energy, forces = pl.pallas_call(
        partial(field_kernel, zcells, xcells, slots, channels, width_x, slabs),
        out_shape=(shape((cells, slots), f32), shape((2, cells, slots), f32)),
        in_specs=[smem()] + [vmem()] * (4 + len(sums)),
        out_specs=(vmem(), vmem()),
        cost_estimate=cost(3_000_000_000, 3_000_000),
    )(place, message, phases, moments, short_energy, *sums)

    return (
        features_out.reshape(features.shape),
        energy.reshape(species.shape),
        forces.reshape(offsets.shape),
    )


def solution(mesh):
    in_specs = (
        P(("groups", "gz"), "xy", None, None),
        P(("groups", "gz"), "xy", None),
        P(("groups", "gz"), "xy", None),
        P(None, ("groups", "gz"), "xy", None),
        P(("groups", "gz"), "xy", None, None),
        P(("groups", "gz"), "xy", None),
        P(("groups", "gz"), "xy", None, None),
        P(),
        P(),
        P(),
        P(),
        P(),
        P(),
        P(),
    )
    out_specs = (
        P(("groups", "gz"), "xy", None, None),
        P(("groups", "gz"), "xy", None),
        P(None, ("groups", "gz"), "xy", None),
    )
    return jax.shard_map(shards, mesh=mesh, in_specs=in_specs, out_specs=out_specs, check_vma=False)
```

```python
import math

import jax
import jax.numpy as jnp
from jax import lax
from jax.experimental import pallas as pl
from jax.experimental.pallas import tpu as pltpu
from jax.sharding import PartitionSpec as P

KX = 128
KY = 8

cell_width = 11.0
layer_depth = 5.5
screening = 0.025
smearing = 1.0
coupling = 0.25
cutoff = 8.0
basis_width = 1.0

HALF_X = KX // 2
HALF_Y = KY // 2
WAVES = 640

f32 = jnp.float32
bf16 = jnp.bfloat16

SIN_TERMS = (9.99999996e-01, -1.66666580e-01, 8.33305062e-03, -1.98090464e-04, 2.60516628e-06)
COS_TERMS = (9.99999953e-01, -4.99999051e-01, 4.16635789e-02, -1.38536669e-03, 2.31531742e-05)


def nt_dot(a, b):
    return lax.dot_general(a, b, (((1,), (1,)), ((), ())), preferred_element_type=f32)


def nn_dot(a, b):
    return lax.dot_general(a, b, (((1,), (0,)), ((), ())), preferred_element_type=f32)


def tn_dot(a, b):
    return lax.dot_general(a, b, (((0,), (0,)), ((), ())), preferred_element_type=f32)


def polynomial(z, terms):
    value = jnp.full_like(z, terms[-1])
    for term in terms[-2::-1]:
        value = value * z + term
    return value


def cos_sin(angle):
    turns = jnp.floor(angle * (1.0 / (2.0 * math.pi)) + 0.5)
    head = 6.28125
    rest = (angle - turns * head) - turns * (2.0 * math.pi - head)
    half = rest * 0.5
    z = half * half
    s = half * polynomial(z, SIN_TERMS)
    c = polynomial(z, COS_TERMS)
    return 1.0 - 2.0 * (s * s), 2.0 * (s * c)


def wave_row(width_x):
    lane = lax.broadcasted_iota(jnp.int32, (1, WAVES), 1)
    block = lane // HALF_X
    place = lane % HALF_X
    edge = block == 2 * HALF_Y + 1
    minus = (block > 0) & (block % 2 == 0)
    step_x = jnp.where(
        edge, jnp.where(place <= HALF_Y, HALF_X, -HALF_X), jnp.where(minus, -place, place)
    )
    step_y = jnp.where(
        edge, jnp.where(place <= HALF_Y, place, place - HALF_Y), (block + 1) // 2
    )
    inner = (place > 0) | ((block > 0) & (step_y < HALF_Y))
    twice = inner & ((step_y < HALF_Y))
    plain = jnp.where(minus & (place == 0), 0, jnp.where(twice, 2, 1))
    count = jnp.where(edge, jnp.where(place < 2 * HALF_Y, 1, 0), plain).astype(f32)
    wave_x = 2.0 * math.pi / width_x * step_x.astype(f32)
    wave_y = 2.0 * math.pi / cell_width * step_y.astype(f32)
    square = wave_x * wave_x + wave_y * wave_y
    screened = jnp.sqrt(square + screening * screening)
    weight = (
        coupling
        * (2.0 * math.pi / (width_x * cell_width))
        * jnp.exp(-0.5 * smearing * smearing * square)
        / screened
    )
    return wave_x, wave_y, screened, weight * count


def twin(row):
    return jnp.concatenate([row, row], axis=1)


def store_phases(out_ref, lanes, coord_x, coord_y, width_x):
    count = coord_x.shape[1]
    step_x = lax.broadcasted_iota(jnp.int32, (HALF_X + 8, count), 0).astype(f32)
    cos_x, sin_x = cos_sin((2.0 * math.pi / width_x * step_x) * coord_x)
    row = lax.broadcasted_iota(jnp.int32, (2 * HALF_Y, count), 0)
    step_y = jnp.where(row <= HALF_Y, row, row - HALF_Y).astype(f32)
    cos_y, sin_y = cos_sin((2.0 * math.pi / cell_width * step_y) * coord_y)
    main_c, main_s = cos_x[:HALF_X], sin_x[:HALF_X]

    def put(block, cosine, sine):
        rows = cosine.shape[0]
        out_ref[block * HALF_X : block * HALF_X + rows, lanes] = cosine.astype(bf16)
        out_ref[WAVES + block * HALF_X : WAVES + block * HALF_X + rows, lanes] = sine.astype(bf16)

    put(0, main_c, main_s)
    for b in range(1, HALF_Y + 1):
        cb, sb = cos_y[b : b + 1], sin_y[b : b + 1]
        cc, ss, sc, cs = main_c * cb, main_s * sb, main_s * cb, main_c * sb
        put(2 * b - 1, cc - ss, sc + cs)
        put(2 * b, cc + ss, cs - sc)
    edge_c = cos_x[HALF_X : HALF_X + 1]
    edge_s = jnp.where(row <= HALF_Y, sin_x[HALF_X : HALF_X + 1], -sin_x[HALF_X : HALF_X + 1])
    blank = jnp.zeros((HALF_X - 2 * HALF_Y, count), f32)
    put(
        2 * HALF_Y + 1,
        jnp.concatenate([edge_c * cos_y - edge_s * sin_y, blank], axis=0),
        jnp.concatenate([edge_s * cos_y + edge_c * sin_y, blank], axis=0),
    )


def layer_charges(charges, sub):
    return jnp.concatenate(
        [
            jnp.where(sub == 0.0, charges, 0.0).astype(bf16),
            jnp.where(sub == 1.0, charges, 0.0).astype(bf16),
        ],
        axis=0,
    )


def lane_rows(read, cells, slots):
    per = 128 // slots
    cat = jnp.concatenate(
        [read(pl.ds(j, cells // per, stride=per)) for j in range(per)], axis=1
    )
    return jnp.concatenate([cat[q : q + 1] for q in range(cells // per)], axis=1)


def three_parts(value):
    head = value.astype(bf16).astype(f32)
    middle = (value - head).astype(bf16).astype(f32)
    return [head, middle, (value - head) - middle]


def start_kernel(zcells, xcells, slots, feat_ref, spec_ref, sub_ref, off_ref, table_ref,
                 cw_ref, hid_ref, msg_ref, right_ref, left_ref):
    cells = zcells * xcells
    atoms = cells * slots
    kinds = table_ref.shape[0]
    spec = lane_rows(lambda rows: spec_ref[rows, :], cells, slots)
    onehot = (lax.broadcasted_iota(jnp.int32, (kinds, atoms), 0) == spec).astype(f32)
    embedded = tn_dot(onehot, table_ref[...].astype(f32))
    hidden = (feat_ref[...].astype(f32) + embedded).astype(bf16)
    hid_ref[...] = hidden
    charges = nt_dot(cw_ref[...], hidden).astype(bf16)
    channels = charges.shape[0]
    sub = lane_rows(lambda rows: sub_ref[rows, :], cells, slots).astype(f32)
    lane_cell = lax.broadcasted_iota(jnp.int32, (1, atoms), 1) // slots % xcells
    cell_x = (lax.axis_index("xy") * xcells + lane_cell).astype(f32)
    coord_x = cell_width * cell_x + lane_rows(lambda rows: off_ref[0, rows, :], cells, slots)
    coord_y = lane_rows(lambda rows: off_ref[1, rows, :], cells, slots)
    extra = jnp.concatenate(
        three_parts(coord_x)
        + three_parts(coord_y)
        + [sub, jnp.zeros((16 - 7, atoms), f32)],
        axis=0,
    ).astype(bf16)
    msg_ref[0:channels, :] = charges
    msg_ref[channels : channels + 16, :] = extra
    for ref, column in ((right_ref, xcells - 1), (left_ref, 0)):
        ref[0:channels, :] = charges
        ref[channels : channels + 16, :] = extra
        for z in range(zcells):
            for h in range(slots // 16):
                begin = (z * xcells + column) * slots + 16 * h
                lane = (z * (slots // 16) + h) * 128
                ref[channels + 16 : channels + 32, lane : lane + 128] = hid_ref[
                    begin : begin + 16, :
                ]


def read_atoms(msg_ref, channels, lanes):
    charges = msg_ref[0:channels, lanes].astype(f32)
    extra = msg_ref[channels : channels + 16, lanes].astype(f32)
    coord_x = (extra[0:1] + extra[1:2]) + extra[2:3]
    coord_y = (extra[3:4] + extra[4:5]) + extra[5:6]
    return charges, coord_x, coord_y, extra[6:7]


def own_kernel(zcells, channels, width_x, msg_ref, phase_ref, moment_ref):
    row_atoms = msg_ref.shape[1] // zcells
    for z in range(zcells):
        lanes = slice(z * row_atoms, (z + 1) * row_atoms)
        charges, coord_x, coord_y, sub = read_atoms(msg_ref, channels, lanes)
        store_phases(phase_ref, lanes, coord_x, coord_y, width_x)
        moment_ref[z] = nt_dot(layer_charges(charges, sub), phase_ref[:, lanes])


def slab_kernel(zcells, channels, width_x, slabs, others, own_ref, *refs):
    msg_refs = refs[:others]
    moment_ref = refs[others]
    send_refs = refs[others + 1 : others + slabs]
    scratch = refs[others + slabs]
    row_atoms = msg_refs[0].shape[1] // zcells
    for z in range(zcells):
        total = own_ref[z]
        for ref in msg_refs:
            lanes = slice(z * row_atoms, (z + 1) * row_atoms)
            charges, coord_x, coord_y, sub = read_atoms(ref, channels, lanes)
            store_phases(scratch, slice(0, row_atoms), coord_x, coord_y, width_x)
            total = total + nt_dot(layer_charges(charges, sub), scratch[...])
        moment_ref[z] = total
    screened = wave_row(width_x)[2]
    decay = twin(jnp.exp(-screened * layer_depth))
    layers = [
        moment_ref[z, l * channels : (l + 1) * channels, :] for z in range(zcells) for l in range(2)
    ]
    top = layers[0]
    for layer in layers[1:]:
        top = decay * top + layer
    bottom = decay * layers[-1]
    for layer in layers[-2::-1]:
        bottom = decay * (bottom + layer)
    for shift, ref in enumerate(send_refs, start=1):
        ref[...] = jnp.where(lax.axis_index("gz") + shift < slabs, top, bottom)


def prepare_kernel(slots, near_ref, dist_ref, count_ref, rin_ref, table_ref, weight_ref, filter_ref):
    cells, _, listed = near_ref.shape
    basis = rin_ref.shape[0]
    groups = 128 // slots
    rows = listed // groups
    rin_t = (0.5 * rin_ref[...].astype(f32)).T.astype(bf16)
    centre = (
        cutoff * lax.broadcasted_iota(jnp.int32, (basis, 256), 0).astype(f32) / (basis - 1)
    )
    lane8 = lax.broadcasted_iota(jnp.int32, (rows, 128), 1)
    slot8 = lane8 % slots
    listed8 = (lane8 // slots) * rows + lax.broadcasted_iota(jnp.int32, (rows, 128), 0)

    def edge_rows(block):
        turned = block.T
        return jnp.concatenate(
            [turned[g * rows : (g + 1) * rows] for g in range(groups)], axis=1
        )

    def one_cell(cell, carry):
        near = edge_rows(near_ref[cell].astype(f32)).astype(jnp.int32)
        dist = edge_rows(dist_ref[cell])
        count = jnp.concatenate([count_ref[pl.ds(cell, 1), :]] * groups, axis=1)
        usable = (listed8 < count) & jnp.logical_not(near == 4 * slots + slot8)
        part = 1.0 - jnp.square(dist * (1.0 / cutoff))
        table_ref[cell] = near
        weight_ref[cell] = jnp.where(usable, part * part, 0.0)
        for q in range(0, rows, 2):
            gap = jnp.concatenate([dist[q : q + 1], dist[q + 1 : q + 2]], axis=1) - centre
            gap = gap / basis_width
            radial = jnp.exp(-(gap * gap)).astype(bf16)
            half = nn_dot(rin_t, radial)
            filter_ref[cell, :, 128 * q : 128 * q + 256] = (half + half * jnp.tanh(half)).astype(
                bf16
            )
        return carry

    lax.fori_loop(0, cells, one_cell, 0, unroll=4)


def extend_kernel(zcells, xcells, slots, channels, hid_ref, left_ref, right_ref, top_ref, bottom_ref):
    count = xcells * slots
    for ref, z in ((top_ref, zcells - 1), (bottom_ref, 0)):
        ref[slots : slots + count, :] = hid_ref[z * count : (z + 1) * count, :]
        for h in range(slots // 16):
            lane = (z * (slots // 16) + h) * 128
            rows = slice(channels + 16, channels + 32)
            ref[16 * h : 16 * h + 16, :] = left_ref[rows, lane : lane + 128]
            begin = slots + count + 16 * h
            ref[begin : begin + 16, :] = right_ref[rows, lane : lane + 128]


def edge_kernel(zcells, xcells, slots, channels, slabs, hid_ref, below_ref, above_ref, left_ref,
                right_ref, table_ref, weight_ref, filter_ref, rout_ref, uin_ref, uout_ref, ew_ref,
                out_ref, energy_ref, ext_ref, rows_a, rows_b, hot_a, hot_b, both_a, both_b, wide_a,
                wide_b, agg_ref):
    features = hid_ref.shape[1]
    wide = (xcells + 2) * slots
    cells = zcells * xcells
    place = lax.axis_index("gz")
    ext_ref[0] = jnp.where(place > 0, below_ref[...], jnp.zeros_like(below_ref))
    ext_ref[zcells + 1] = jnp.where(place < slabs - 1, above_ref[...], jnp.zeros_like(above_ref))
    for z in range(zcells):
        ext_ref[z + 1, slots : slots + xcells * slots, :] = hid_ref[
            z * xcells * slots : (z + 1) * xcells * slots, :
        ]
        for h in range(slots // 16):
            lane = (z * (slots // 16) + h) * 128
            ext_ref[z + 1, 16 * h : 16 * h + 16, :] = left_ref[
                channels + 16 : channels + 32, lane : lane + 128
            ]
            ext_ref[z + 1, wide - slots + 16 * h : wide - slots + 16 * h + 16, :] = right_ref[
                channels + 16 : channels + 32, lane : lane + 128
            ]
    rout_t = rout_ref[...].astype(f32).T.astype(bf16)
    uin_t = (0.5 * uin_ref[...].astype(f32)).T.astype(bf16)
    groups = 128 // slots
    chunks = table_ref.shape[1] // 2
    region = 9 * slots // 2
    row_id = lax.broadcasted_iota(jnp.int32, (16, 256), 0).astype(jnp.int16)
    one, zero = jnp.ones((16, 256), bf16), jnp.zeros((16, 256), bf16)
    group_lane = lax.broadcasted_iota(jnp.int32, (features, 128), 1) // slots

    def pair(table, q):
        return jnp.concatenate([table[2 * q : 2 * q + 1], table[2 * q + 1 : 2 * q + 2]], axis=1)

    def make_hot(cell, hot_ref, rows_ref):
        near = table_ref[cell]
        index = jnp.where(near >= region, near - region, near)
        for q in range(chunks):
            column = jnp.broadcast_to(pair(index, q), (16, 256)).astype(jnp.int16)
            for r in range(0, region, 16):
                hot_ref[q, r : r + 16, :] = jnp.where(column == row_id + r, one, zero)
        z = cell // xcells
        begin = pl.multiple_of(cell % xcells * slots, slots)
        rows = jnp.concatenate(
            [ext_ref[z + dz, pl.ds(begin, 3 * slots), :] for dz in range(3)], axis=0
        )
        rows_ref[:features] = rows[:region].astype(f32).T.astype(bf16)
        rows_ref[features:] = rows[region:].astype(f32).T.astype(bf16)

    def multiply(cell, hot_ref, rows_ref, both_ref, wide_ref):
        rows_t = rows_ref[...]
        for q in range(chunks):
            both_ref[q] = nn_dot(rows_t, hot_ref[q])
            wide_ref[q] = nn_dot(rout_t, filter_ref[cell, :, 256 * q : 256 * q + 256])

    def gather_up(cell, both_ref, wide_ref):
        near = table_ref[cell]
        weight = weight_ref[cell]
        total = jnp.zeros((features, 128), f32)
        for q in range(chunks):
            upper = pair(near, q) >= region
            picked = jnp.where(upper, both_ref[q, features:], both_ref[q, :features])
            product = (pair(weight, q) * wide_ref[q]) * picked
            total = total + (product[:, :128] + product[:, 128:])
        shift = 64
        while shift >= slots:
            total = total + pltpu.roll(total, shift, 1)
            shift //= 2
        step = cell // groups
        agg_ref[step] = jnp.where(group_lane == cell % groups, total, agg_ref[step])

    make_hot(0, hot_a, rows_a)

    def two_cells(turn, carry):
        cell = 2 * turn
        multiply(cell, hot_a, rows_a, both_a, wide_a)
        make_hot(cell + 1, hot_b, rows_b)
        gather_up(jnp.maximum(cell - 1, 0), both_b, wide_b)
        multiply(cell + 1, hot_b, rows_b, both_b, wide_b)
        make_hot(jnp.minimum(cell + 2, cells - 1), hot_a, rows_a)
        gather_up(cell, both_a, wide_a)
        return carry

    lax.fori_loop(0, cells // 2, two_cells, 0)
    gather_up(cells - 1, both_b, wide_b)

    for step in range(cells // groups):
        half = nn_dot(uin_t, agg_ref[step].astype(bf16))
        hidden = (half + half * jnp.tanh(half)).T.astype(bf16)
        begin = step * 128
        renewed = hid_ref[begin : begin + 128, :].astype(f32) + nn_dot(hidden, uout_ref[...])
        out_ref[begin : begin + 128, :] = renewed.astype(bf16)
        weighted = renewed * ew_ref[...].astype(f32)
        energy_ref[step : step + 1, :] = jnp.sum(weighted.T, axis=0, keepdims=True)


def field_kernel(zcells, xcells, slots, channels, width_x, slabs, msg_ref, phase_ref, moment_ref,
                 short_ref, *refs):
    sums = refs[: slabs - 1]
    energy_ref, force_ref = refs[slabs - 1 :]
    wave_x, wave_y, screened, weight = wave_row(width_x)
    decay = twin(jnp.exp(-screened * layer_depth))
    span = decay
    for _ in range(2 * zcells - 1):
        span = span * decay
    place = lax.axis_index("gz")
    below = jnp.zeros_like(sums[0][...])
    above = jnp.zeros_like(below)
    for shift in range(slabs - 1, 0, -1):
        below = jnp.where(place >= shift, below * span + sums[shift - 1][...], below)
    for shift in range(1, slabs):
        above = jnp.where(place < shift, above * span + sums[shift - 1][...], above)
    layers = [
        moment_ref[z, l * channels : (l + 1) * channels, :] for z in range(zcells) for l in range(2)
    ]
    down = []
    for layer in layers:
        below = decay * below + layer
        down.append(below)
    up = [above]
    for layer in layers[:0:-1]:
        above = decay * (above + layer)
        up.append(above)
    up = up[::-1]
    row_atoms = xcells * slots
    for z in range(zcells):
        lanes = slice(z * row_atoms, (z + 1) * row_atoms)
        rows = []
        for l in range(2):
            field = down[2 * z + l] + up[2 * z + l]
            cosine = field[:, :WAVES] * weight
            sine = field[:, WAVES:] * weight
            rows.append(jnp.concatenate([cosine, sine], axis=1))
            rows.append(jnp.concatenate([wave_x * sine, -wave_x * cosine], axis=1))
            rows.append(jnp.concatenate([wave_y * sine, -wave_y * cosine], axis=1))
        panel = jnp.concatenate([row.astype(bf16) for row in rows], axis=0)
        evaluated = nn_dot(panel, phase_ref[:, lanes])
        sub = msg_ref[channels : channels + 16, lanes].astype(f32)[6:7]
        chosen = jnp.where(sub == 0.0, evaluated[: 3 * channels], evaluated[3 * channels :])
        charges = msg_ref[0:channels, lanes].astype(f32)
        long_energy = 0.5 * jnp.sum(charges * chosen[:channels], axis=0, keepdims=True)
        force_x = -jnp.sum(charges * chosen[channels : 2 * channels], axis=0, keepdims=True)
        force_y = -jnp.sum(charges * chosen[2 * channels :], axis=0, keepdims=True)
        per = row_atoms // 128
        short = jnp.concatenate(
            [short_ref[z * per + j : z * per + j + 1, :] for j in range(per)], axis=1
        )
        energy = short + long_energy
        for x in range(xcells):
            cell = z * xcells + x
            piece = slice(x * slots, (x + 1) * slots)
            energy_ref[cell : cell + 1, :] = energy[:, piece]
            force_ref[0, cell : cell + 1, :] = force_x[:, piece]
            force_ref[1, cell : cell + 1, :] = force_y[:, piece]


def vmem():
    return pl.BlockSpec(memory_space=pltpu.VMEM)


def hbm():
    return pl.BlockSpec(memory_space=pltpu.HBM)


def fetching(body, count):
    def kernel(*refs):
        copies, sems = refs[-count - 1 : -1], refs[-1]
        moves = [
            pltpu.make_async_copy(refs[i], copies[i], sems.at[i]) for i in range(count)
        ]
        for move in moves:
            move.start()
        for move in moves:
            move.wait()
        body(*copies, *refs[count : -count - 1])

    kernel.__name__ = body.__name__
    return kernel


def held(arrays):
    return [pltpu.with_memory_space_constraint(a, pltpu.HBM) for a in arrays]


def fetch_scratch(arrays):
    return [pltpu.VMEM(a.shape, a.dtype) for a in arrays] + [
        pltpu.SemaphoreType.DMA((len(arrays),))
    ]


def shards(
    features,
    species,
    sublayer,
    offsets,
    neighbours,
    neighbour_count,
    distances,
    species_table,
    charge_weight,
    radial_in,
    radial_out,
    update_in,
    update_out,
    energy_weight,
):
    zcells, xcells, slots, width = features.shape
    channels = charge_weight.shape[1]
    listed = neighbours.shape[3]
    cells = zcells * xcells
    atoms = cells * slots
    strips = lax.axis_size("xy")
    slabs = lax.axis_size("gz")
    width_x = cell_width * (xcells * strips)

    def shape(dims, kind):
        return jax.ShapeDtypeStruct(dims, kind)

    def partial(body, *static):
        def kernel(*refs):
            body(*static, *refs)

        kernel.__name__ = body.__name__
        return kernel

    def grant(mebibytes):
        return pltpu.CompilerParams(vmem_limit_bytes=mebibytes * 1024 * 1024)

    def cost(flops, data):
        return pl.CostEstimate(flops=flops, bytes_accessed=data, transcendentals=0)

    inputs = (
        features.reshape(atoms, width),
        species.reshape(cells, slots),
        sublayer.reshape(cells, slots),
        offsets.reshape(2, cells, slots),
        species_table,
        charge_weight.T,
    )
    hidden, message, to_right, to_left = pl.pallas_call(
        fetching(partial(start_kernel, zcells, xcells, slots), len(inputs)),
        out_shape=(
            shape((atoms, width), bf16),
            shape((channels + 16, atoms), bf16),
            shape((channels + 32, atoms), bf16),
            shape((channels + 32, atoms), bf16),
        ),
        in_specs=[hbm()] * len(inputs),
        out_specs=(vmem(),) * 4,
        scratch_shapes=fetch_scratch(inputs),
        compiler_params=grant(6),
    )(*held(inputs))

    def ring(count, shift):
        return [(i, (i + shift) % count) for i in range(count)]

    from_left = lax.ppermute(to_right, "xy", ring(strips, 1))
    from_right = lax.ppermute(to_left, "xy", ring(strips, strips - 1))
    messages = [from_left, from_right] + [
        lax.ppermute(message, "xy", ring(strips, shift)) for shift in range(2, strips - 1)
    ]

    phases, own_moments = pl.pallas_call(
        partial(own_kernel, zcells, channels, width_x),
        out_shape=(
            shape((2 * WAVES, atoms), bf16),
            shape((zcells, 2 * channels, 2 * WAVES), f32),
        ),
        in_specs=[vmem()],
        out_specs=(vmem(), vmem()),
        compiler_params=grant(8),
        cost_estimate=cost(4_000_000_000, 2_000_000),
    )(message)

    rows = listed * slots // 128
    chunks = rows // 2
    inputs = (
        neighbours.reshape(cells, slots, listed),
        distances.reshape(cells, slots, listed),
        neighbour_count.reshape(cells, slots),
        radial_in,
    )
    table, weight, filters = pl.pallas_call(
        fetching(partial(prepare_kernel, slots), len(inputs)),
        out_shape=(
            shape((cells, rows, 128), jnp.int32),
            shape((cells, rows, 128), f32),
            shape((cells, radial_in.shape[1], rows * 128), bf16),
        ),
        in_specs=[hbm()] * len(inputs),
        out_specs=(vmem(),) * 3,
        scratch_shapes=fetch_scratch(inputs),
        compiler_params=grant(10),
        cost_estimate=cost(6_000_000_000, 4_000_000),
    )(*held(inputs))

    slab = pl.pallas_call(
        partial(slab_kernel, zcells, channels, width_x, slabs, len(messages)),
        out_shape=(shape((zcells, 2 * channels, 2 * WAVES), f32),)
        + (shape((channels, 2 * WAVES), f32),) * (slabs - 1),
        in_specs=[vmem()] * (1 + len(messages)),
        out_specs=(vmem(),) * slabs,
        scratch_shapes=[pltpu.VMEM((2 * WAVES, atoms // zcells), bf16)],
        compiler_params=grant(8),
        cost_estimate=cost(8_000_000_000, 2_000_000),
    )(own_moments, *messages)
    moments = slab[0]

    wide = ((xcells + 2) * slots, width)
    top, bottom = pl.pallas_call(
        partial(extend_kernel, zcells, xcells, slots, channels),
        out_shape=(shape(wide, bf16), shape(wide, bf16)),
        in_specs=[vmem()] * 3,
        out_specs=(vmem(), vmem()),
        compiler_params=grant(4),
    )(hidden, from_left, from_right)
    below = lax.ppermute(top, "gz", ring(slabs, 1))
    above = lax.ppermute(bottom, "gz", ring(slabs, slabs - 1))
    sums = [
        lax.ppermute(slab[shift], "gz", ring(slabs, shift)) for shift in range(1, slabs)
    ]

    features_out, short_energy = pl.pallas_call(
        partial(edge_kernel, zcells, xcells, slots, channels, slabs),
        out_shape=(shape((atoms, width), bf16), shape((atoms // 128, 128), f32)),
        in_specs=[vmem()] * 12,
        out_specs=(vmem(), vmem()),
        scratch_shapes=[
            pltpu.VMEM((zcells + 2, (xcells + 2) * slots, width), bf16),
            pltpu.VMEM((2 * width, 9 * slots // 2), bf16),
            pltpu.VMEM((2 * width, 9 * slots // 2), bf16),
            pltpu.VMEM((chunks, 9 * slots // 2, 256), bf16),
            pltpu.VMEM((chunks, 9 * slots // 2, 256), bf16),
            pltpu.VMEM((chunks, 2 * width, 256), f32),
            pltpu.VMEM((chunks, 2 * width, 256), f32),
            pltpu.VMEM((chunks, width, 256), f32),
            pltpu.VMEM((chunks, width, 256), f32),
            pltpu.VMEM((atoms // 128, width, 128), f32),
        ],
        compiler_params=grant(16),
        cost_estimate=cost(12_000_000_000, 4_000_000),
    )(
        hidden,
        below,
        above,
        from_left,
        from_right,
        table,
        weight,
        filters,
        radial_out,
        update_in,
        update_out,
        energy_weight.reshape(1, width),
    )

    energy, forces = pl.pallas_call(
        partial(field_kernel, zcells, xcells, slots, channels, width_x, slabs),
        out_shape=(shape((cells, slots), f32), shape((2, cells, slots), f32)),
        in_specs=[vmem()] * (4 + len(sums)),
        out_specs=(vmem(), vmem()),
        compiler_params=grant(8),
        cost_estimate=cost(3_000_000_000, 3_000_000),
    )(message, phases, moments, short_energy, *sums)

    return (
        features_out.reshape(features.shape),
        energy.reshape(species.shape),
        forces.reshape(offsets.shape),
    )


def solution(mesh):
    in_specs = (
        P(("groups", "gz"), "xy", None, None),
        P(("groups", "gz"), "xy", None),
        P(("groups", "gz"), "xy", None),
        P(None, ("groups", "gz"), "xy", None),
        P(("groups", "gz"), "xy", None, None),
        P(("groups", "gz"), "xy", None),
        P(("groups", "gz"), "xy", None, None),
        P(),
        P(),
        P(),
        P(),
        P(),
        P(),
        P(),
    )
    out_specs = (
        P(("groups", "gz"), "xy", None, None),
        P(("groups", "gz"), "xy", None),
        P(None, ("groups", "gz"), "xy", None),
    )
    return jax.shard_map(shards, mesh=mesh, in_specs=in_specs, out_specs=out_specs, check_vma=False)
```

```python
import math

import jax
import jax.numpy as jnp
from jax import lax
from jax.experimental import pallas as pl
from jax.experimental.pallas import tpu as pltpu
from jax.sharding import PartitionSpec as P

KX = 128
KY = 8

cell_width = 11.0
layer_depth = 5.5
screening = 0.025
smearing = 1.0
coupling = 0.25
cutoff = 8.0
basis_width = 1.0

HALF_X = KX // 2
HALF_Y = KY // 2
WAVES = 640

f32 = jnp.float32
bf16 = jnp.bfloat16

SIN_TERMS = (9.99999996e-01, -1.66666580e-01, 8.33305062e-03, -1.98090464e-04, 2.60516628e-06)
COS_TERMS = (9.99999953e-01, -4.99999051e-01, 4.16635789e-02, -1.38536669e-03, 2.31531742e-05)


def nt_dot(a, b):
    return lax.dot_general(a, b, (((1,), (1,)), ((), ())), preferred_element_type=f32)


def nn_dot(a, b):
    return lax.dot_general(a, b, (((1,), (0,)), ((), ())), preferred_element_type=f32)


def tn_dot(a, b):
    return lax.dot_general(a, b, (((0,), (0,)), ((), ())), preferred_element_type=f32)


def polynomial(z, terms):
    value = jnp.full_like(z, terms[-1])
    for term in terms[-2::-1]:
        value = value * z + term
    return value


def cos_sin(angle):
    turns = jnp.floor(angle * (1.0 / (2.0 * math.pi)) + 0.5)
    head = 6.28125
    rest = (angle - turns * head) - turns * (2.0 * math.pi - head)
    half = rest * 0.5
    z = half * half
    s = half * polynomial(z, SIN_TERMS)
    c = polynomial(z, COS_TERMS)
    return 1.0 - 2.0 * (s * s), 2.0 * (s * c)


def wave_row(width_x):
    lane = lax.broadcasted_iota(jnp.int32, (1, WAVES), 1)
    block = lane // HALF_X
    place = lane % HALF_X
    edge = block == 2 * HALF_Y + 1
    minus = (block > 0) & (block % 2 == 0)
    step_x = jnp.where(
        edge, jnp.where(place <= HALF_Y, HALF_X, -HALF_X), jnp.where(minus, -place, place)
    )
    step_y = jnp.where(
        edge, jnp.where(place <= HALF_Y, place, place - HALF_Y), (block + 1) // 2
    )
    inner = (place > 0) | ((block > 0) & (step_y < HALF_Y))
    twice = inner & ((step_y < HALF_Y))
    plain = jnp.where(minus & (place == 0), 0, jnp.where(twice, 2, 1))
    count = jnp.where(edge, jnp.where(place < 2 * HALF_Y, 1, 0), plain).astype(f32)
    wave_x = 2.0 * math.pi / width_x * step_x.astype(f32)
    wave_y = 2.0 * math.pi / cell_width * step_y.astype(f32)
    square = wave_x * wave_x + wave_y * wave_y
    screened = jnp.sqrt(square + screening * screening)
    weight = (
        coupling
        * (2.0 * math.pi / (width_x * cell_width))
        * jnp.exp(-0.5 * smearing * smearing * square)
        / screened
    )
    return wave_x, wave_y, screened, weight * count


def twin(row):
    return jnp.concatenate([row, row], axis=1)


def store_phases(out_ref, lanes, coord_x, coord_y, width_x):
    count = coord_x.shape[1]
    row = lax.broadcasted_iota(jnp.int32, (8, count), 0)
    step_y = jnp.where(row <= HALF_Y, row, row - HALF_Y).astype(f32)
    unit_x = 2.0 * math.pi / width_x * row.astype(f32)
    cosine, sine = cos_sin(
        jnp.concatenate(
            [
                unit_x * coord_x,
                (8.0 * unit_x) * coord_x,
                (2.0 * math.pi / cell_width * step_y) * coord_y,
            ],
            axis=0,
        )
    )
    fine_c, fine_s = cosine[:8], sine[:8]
    cos_y, sin_y = cosine[16:], sine[16:]
    main_c, main_s = [fine_c], [fine_s]
    for h in range(1, HALF_X // 8):
        hc, hs = cosine[8 + h : 9 + h], sine[8 + h : 9 + h]
        main_c.append(hc * fine_c - hs * fine_s)
        main_s.append(hs * fine_c + hc * fine_s)
    last_c, last_s = cosine[7 + HALF_X // 8 : 8 + HALF_X // 8], sine[7 + HALF_X // 8 : 8 + HALF_X // 8]
    edge_c = last_c * cosine[9:10] - last_s * sine[9:10]
    edge_s = last_s * cosine[9:10] + last_c * sine[9:10]
    main_c, main_s = jnp.concatenate(main_c, axis=0), jnp.concatenate(main_s, axis=0)

    def put(block, cosine, sine):
        rows = cosine.shape[0]
        out_ref[block * HALF_X : block * HALF_X + rows, lanes] = cosine.astype(bf16)
        out_ref[WAVES + block * HALF_X : WAVES + block * HALF_X + rows, lanes] = sine.astype(bf16)

    put(0, main_c, main_s)
    for b in range(1, HALF_Y + 1):
        cb, sb = cos_y[b : b + 1], sin_y[b : b + 1]
        cc, ss, sc, cs = main_c * cb, main_s * sb, main_s * cb, main_c * sb
        put(2 * b - 1, cc - ss, sc + cs)
        put(2 * b, cc + ss, cs - sc)
    edge_s = jnp.where(row <= HALF_Y, edge_s, -edge_s)
    blank = jnp.zeros((HALF_X - 2 * HALF_Y, count), f32)
    put(
        2 * HALF_Y + 1,
        jnp.concatenate([edge_c * cos_y - edge_s * sin_y, blank], axis=0),
        jnp.concatenate([edge_s * cos_y + edge_c * sin_y, blank], axis=0),
    )


def layer_charges(charges, sub):
    return jnp.concatenate(
        [
            jnp.where(sub == 0.0, charges, 0.0).astype(bf16),
            jnp.where(sub == 1.0, charges, 0.0).astype(bf16),
        ],
        axis=0,
    )


def lane_rows(read, cells, slots):
    per = 128 // slots
    cat = jnp.concatenate(
        [read(pl.ds(j, cells // per, stride=per)) for j in range(per)], axis=1
    )
    return jnp.concatenate([cat[q : q + 1] for q in range(cells // per)], axis=1)


def three_parts(value):
    head = value.astype(bf16).astype(f32)
    middle = (value - head).astype(bf16).astype(f32)
    return [head, middle, (value - head) - middle]


def start_kernel(zcells, xcells, slots, feat_ref, spec_ref, sub_ref, off_ref, table_ref,
                 cw_ref, hid_ref, msg_ref, even_ref, odd_ref):
    cells = zcells * xcells
    atoms = cells * slots
    kinds = table_ref.shape[0]
    spec = lane_rows(lambda rows: spec_ref[rows, :], cells, slots)
    onehot = (lax.broadcasted_iota(jnp.int32, (kinds, atoms), 0) == spec).astype(f32)
    embedded = tn_dot(onehot, table_ref[...].astype(f32))
    hidden = (feat_ref[...].astype(f32) + embedded).astype(bf16)
    hid_ref[...] = hidden
    charges = nt_dot(cw_ref[...], hidden).astype(bf16)
    channels = charges.shape[0]
    sub = lane_rows(lambda rows: sub_ref[rows, :], cells, slots).astype(f32)
    lane_cell = lax.broadcasted_iota(jnp.int32, (1, atoms), 1) // slots % xcells
    cell_x = (lax.axis_index("xy") * xcells + lane_cell).astype(f32)
    coord_x = cell_width * cell_x + lane_rows(lambda rows: off_ref[0, rows, :], cells, slots)
    coord_y = lane_rows(lambda rows: off_ref[1, rows, :], cells, slots)
    extra = jnp.concatenate(
        three_parts(coord_x)
        + three_parts(coord_y)
        + [sub, jnp.zeros((16 - 7, atoms), f32)],
        axis=0,
    ).astype(bf16)
    msg_ref[0:channels, :] = charges
    msg_ref[channels : channels + 16, :] = extra
    even = lax.axis_index("xy") % 2 == 0
    right = xcells - 1
    for ref, column in ((even_ref, jnp.where(even, right, 0)), (odd_ref, jnp.where(even, 0, right))):
        ref[0:channels, :] = charges
        ref[channels : channels + 16, :] = extra
        for z in range(zcells):
            for h in range(slots // 16):
                begin = pl.multiple_of((z * xcells + column) * slots + 16 * h, 16)
                lane = (z * (slots // 16) + h) * 128
                ref[channels + 16 : channels + 32, lane : lane + 128] = hid_ref[
                    pl.ds(begin, 16), :
                ]


def read_atoms(msg_ref, channels, lanes):
    charges = msg_ref[0:channels, lanes].astype(f32)
    extra = msg_ref[channels : channels + 16, lanes].astype(f32)
    coord_x = (extra[0:1] + extra[1:2]) + extra[2:3]
    coord_y = (extra[3:4] + extra[4:5]) + extra[5:6]
    return charges, coord_x, coord_y, extra[6:7]


def own_kernel(zcells, channels, width_x, slots, near_hbm, dist_hbm, count_hbm, rin_hbm, msg_ref,
               phase_ref, moment_ref, table_ref, weight_ref, filter_ref, near_ref, dist_ref,
               count_ref, rin_ref, rad_a, rad_b, sems):
    moves = [
        pltpu.make_async_copy(source, target, sems.at[i])
        for i, (source, target) in enumerate(
            (
                (near_hbm, near_ref),
                (dist_hbm, dist_ref),
                (count_hbm, count_ref),
                (rin_hbm, rin_ref),
            )
        )
    ]
    for move in moves:
        move.start()
    row_atoms = msg_ref.shape[1] // zcells
    for z in range(zcells):
        lanes = slice(z * row_atoms, (z + 1) * row_atoms)
        charges, coord_x, coord_y, sub = read_atoms(msg_ref, channels, lanes)
        store_phases(phase_ref, lanes, coord_x, coord_y, width_x)
        moment_ref[z] = nt_dot(layer_charges(charges, sub), phase_ref[:, lanes])
    for move in moves:
        move.wait()

    cells, _, listed = near_ref.shape
    basis = rin_ref.shape[0]
    groups = 128 // slots
    rows = listed // groups
    rin_t = (0.5 * rin_ref[...].astype(f32)).T.astype(bf16)
    centre = (
        cutoff * lax.broadcasted_iota(jnp.int32, (basis, 128), 0).astype(f32) / (basis - 1)
    )
    lane8 = lax.broadcasted_iota(jnp.int32, (rows, 128), 1)
    slot8 = lane8 % slots
    listed8 = (lane8 // slots) * rows + lax.broadcasted_iota(jnp.int32, (rows, 128), 0)

    def edge_rows(block):
        turned = block.T
        return jnp.concatenate(
            [turned[g * rows : (g + 1) * rows] for g in range(groups)], axis=1
        )

    def spread(cell, rad_ref, slot):
        near = edge_rows(near_ref[cell].astype(f32)).astype(jnp.int32)
        dist = edge_rows(dist_ref[cell])
        count = jnp.concatenate([count_ref[pl.ds(cell, 1), :]] * groups, axis=1)
        usable = (listed8 < count) & jnp.logical_not(near == 4 * slots + slot8)
        part = 1.0 - jnp.square(dist * (1.0 / cutoff))
        table_ref[cell] = near
        weight_ref[cell] = jnp.where(usable, part * part, 0.0)
        for q in range(rows):
            gap = (dist[q : q + 1] - centre) / basis_width
            rad_ref[slot, :, 128 * q : 128 * q + 128] = jnp.exp(-(gap * gap)).astype(bf16)

    def filtered(cell, rad_ref, slot):
        for q in range(0, rows * 128, 256):
            half = nn_dot(rin_t, rad_ref[slot, :, q : q + 256])
            filter_ref[cell, :, q : q + 256] = (half + half * jnp.tanh(half)).astype(bf16)

    for slot in range(2):
        spread(slot, rad_a, slot)

    def four_cells(turn, carry):
        cell = 4 * turn
        for slot in range(2):
            filtered(cell + slot, rad_a, slot)
            spread(cell + 2 + slot, rad_b, slot)
        for slot in range(2):
            filtered(cell + 2 + slot, rad_b, slot)
            spread(jnp.minimum(cell + 4 + slot, cells - 1), rad_a, slot)
        return carry

    lax.fori_loop(0, cells // 4, four_cells, 0)


def targets(place, count):
    even = place % 2 == 0
    above, below = (place + 1) % count, (place + count - 1) % count
    return [jnp.where(even, above, below), jnp.where(even, below, above)] + [
        (place + shift) % count for shift in range(2, count - 1)
    ]


def routes(count):
    even = [(i, i + 1 if i % 2 == 0 else i - 1) for i in range(count)]
    odd = [(i, (i + 1) % count if i % 2 == 1 else (i - 1) % count) for i in range(count)]
    return [even, odd] + [
        [(i, (i + shift) % count) for i in range(count)] for shift in range(2, count - 1)
    ]


def slab_kernel(zcells, channels, width_x, slabs, others, own_ref, *refs):
    msg_refs = refs[:others]
    moment_ref = refs[others]
    send_refs = refs[others + 1 : others + slabs]
    scratch = refs[others + slabs]
    row_atoms = msg_refs[0].shape[1] // zcells
    for z in range(zcells):
        total = own_ref[z]
        for ref in msg_refs:
            lanes = slice(z * row_atoms, (z + 1) * row_atoms)
            charges, coord_x, coord_y, sub = read_atoms(ref, channels, lanes)
            store_phases(scratch, slice(0, row_atoms), coord_x, coord_y, width_x)
            total = total + nt_dot(layer_charges(charges, sub), scratch[...])
        moment_ref[z] = total
    screened = wave_row(width_x)[2]
    decay = twin(jnp.exp(-screened * layer_depth))
    layers = [
        moment_ref[z, l * channels : (l + 1) * channels, :] for z in range(zcells) for l in range(2)
    ]
    top = layers[0]
    for layer in layers[1:]:
        top = decay * top + layer
    bottom = decay * layers[-1]
    for layer in layers[-2::-1]:
        bottom = decay * (bottom + layer)
    place = lax.axis_index("gz")
    for target, ref in zip(targets(place, slabs), send_refs):
        ref[...] = jnp.where(target > place, top, bottom)


def sides(even_ref, odd_ref, rows, lanes):
    first, second = even_ref[rows, lanes], odd_ref[rows, lanes]
    even = lax.axis_index("xy") % 2 == 0
    return jnp.where(even, second, first), jnp.where(even, first, second)


def fill_row(ref, z, xcells, slots, channels, hid_ref, even_ref, odd_ref):
    count = xcells * slots
    ref[slots : slots + count, :] = hid_ref[z * count : (z + 1) * count, :]
    for h in range(slots // 16):
        lane = (z * (slots // 16) + h) * 128
        left, right = sides(
            even_ref, odd_ref, slice(channels + 16, channels + 32), slice(lane, lane + 128)
        )
        ref[16 * h : 16 * h + 16, :] = left
        begin = slots + count + 16 * h
        ref[begin : begin + 16, :] = right


def extend_kernel(zcells, xcells, slots, channels, hid_ref, even_ref, odd_ref, first_ref,
                  second_ref, ext_ref):
    for z in range(zcells):
        fill_row(ext_ref.at[z], z, xcells, slots, channels, hid_ref, even_ref, odd_ref)
    even = lax.axis_index("gz") % 2 == 0
    first_ref[...] = ext_ref[jnp.where(even, zcells - 1, 0)]
    second_ref[...] = ext_ref[jnp.where(even, 0, zcells - 1)]


def edge_kernel(zcells, xcells, slots, slabs, first_ref, second_ref, own_ref, table_ref, weight_ref,
                filter_ref, rout_ref, agg_ref, ext_ref, rows_a, rows_b, hot_a, hot_b, both_a,
                both_b, wide_a, wide_b):
    features = own_ref.shape[2]
    cells = zcells * xcells
    place = lax.axis_index("gz")
    even = place % 2 == 0
    first, second = first_ref[...], second_ref[...]
    blank = jnp.zeros_like(first)
    ext_ref[0] = jnp.where(place > 0, jnp.where(even, second, first), blank)
    ext_ref[zcells + 1] = jnp.where(place < slabs - 1, jnp.where(even, first, second), blank)
    ext_ref[1 : zcells + 1] = own_ref[...]
    rout_t = rout_ref[...].astype(f32).T.astype(bf16)
    groups = 128 // slots
    chunks = table_ref.shape[1] // 2
    region = 9 * slots // 2
    row_id = lax.broadcasted_iota(jnp.int32, (16, 256), 0).astype(jnp.int16)
    one, zero = jnp.ones((16, 256), bf16), jnp.zeros((16, 256), bf16)
    group_lane = lax.broadcasted_iota(jnp.int32, (features, 128), 1) // slots

    def pair(table, q):
        return jnp.concatenate([table[2 * q : 2 * q + 1], table[2 * q + 1 : 2 * q + 2]], axis=1)

    def make_hot(cell, hot_ref, rows_ref):
        near = table_ref[cell]
        index = jnp.where(near >= region, near - region, near)
        for q in range(chunks):
            column = jnp.broadcast_to(pair(index, q), (16, 256)).astype(jnp.int16)
            for r in range(0, region, 16):
                hot_ref[q, r : r + 16, :] = jnp.where(column == row_id + r, one, zero)
        z = cell // xcells
        begin = pl.multiple_of(cell % xcells * slots, slots)
        rows = jnp.concatenate(
            [ext_ref[z + dz, pl.ds(begin, 3 * slots), :] for dz in range(3)], axis=0
        )
        rows_ref[:features] = rows[:region].astype(f32).T.astype(bf16)
        rows_ref[features:] = rows[region:].astype(f32).T.astype(bf16)

    def multiply(cell, hot_ref, rows_ref, both_ref, wide_ref):
        rows_t = rows_ref[...]
        for q in range(chunks):
            both_ref[q] = nn_dot(rows_t, hot_ref[q])
            wide_ref[q] = nn_dot(rout_t, filter_ref[cell, :, 256 * q : 256 * q + 256])

    def gather_up(cell, both_ref, wide_ref):
        near = table_ref[cell]
        weight = weight_ref[cell]
        total = jnp.zeros((features, 128), f32)
        for q in range(chunks):
            upper = pair(near, q) >= region
            picked = jnp.where(upper, both_ref[q, features:], both_ref[q, :features])
            product = (pair(weight, q) * wide_ref[q]) * picked
            total = total + (product[:, :128] + product[:, 128:])
        shift = 64
        while shift >= slots:
            total = total + pltpu.roll(total, shift, 1)
            shift //= 2
        step = cell // groups
        agg_ref[step] = jnp.where(group_lane == cell % groups, total, agg_ref[step])

    make_hot(0, hot_a, rows_a)

    def four_cells(turn, carry):
        for cell in (4 * turn, 4 * turn + 2):
            multiply(cell, hot_a, rows_a, both_a, wide_a)
            make_hot(cell + 1, hot_b, rows_b)
            gather_up(jnp.maximum(cell - 1, 0), both_b, wide_b)
            multiply(cell + 1, hot_b, rows_b, both_b, wide_b)
            make_hot(jnp.minimum(cell + 2, cells - 1), hot_a, rows_a)
            gather_up(cell, both_a, wide_a)
        return carry

    lax.fori_loop(0, cells // 4, four_cells, 0)
    gather_up(cells - 1, both_b, wide_b)


def field_kernel(zcells, xcells, slots, channels, width_x, slabs, msg_ref, phase_ref, moment_ref,
                 hid_ref, agg_ref, uin_ref, uout_ref, ew_ref, *refs):
    sums = [ref[...] for ref in refs[: slabs - 1]]
    out_ref, energy_ref, force_ref = refs[slabs - 1 :]

    aggregate = jnp.concatenate(
        [agg_ref[step].astype(bf16) for step in range(agg_ref.shape[0])], axis=1
    )
    uin_t = (0.5 * uin_ref[...].astype(f32)).T.astype(bf16)
    uout_t = uout_ref[...].astype(f32).T.astype(bf16)
    half = nn_dot(uin_t, aggregate)
    update = nn_dot(uout_t, (half + half * jnp.tanh(half)).astype(bf16))
    readout = ew_ref[...]
    energy_column = jnp.broadcast_to(readout.astype(f32), (8, readout.shape[1])).T[:, :1]
    short = jnp.sum(update * energy_column, axis=0, keepdims=True) + nt_dot(
        jnp.broadcast_to(readout, (16, readout.shape[1])), hid_ref[...]
    )[:1]
    out_ref[...] = (hid_ref[...].astype(f32) + update.T).astype(bf16)

    wave_x, wave_y, screened, weight = wave_row(width_x)
    decay = twin(jnp.exp(-screened * layer_depth))
    span = decay
    for _ in range(2 * zcells - 1):
        span = span * decay
    spans = [jnp.ones_like(span)]
    for _ in range(slabs - 2):
        spans.append(spans[-1] * span)
    place = lax.axis_index("gz")
    even = place % 2 == 0
    inner = jnp.where(even, place > 0, place < slabs - 1)
    near, other = sums[0], sums[1]
    other = jnp.where(inner, other, other * spans[-1])
    other_below = jnp.where(even, place > 0, place == slabs - 1)
    zero = jnp.zeros_like(near)
    below = jnp.where(even, zero, near) + jnp.where(other_below, other, zero)
    above = jnp.where(even, near, zero) + jnp.where(other_below, zero, other)
    for shift, value in enumerate(sums[2:], start=2):
        under = place >= shift
        value = value * jnp.where(under, spans[shift - 1], spans[slabs - shift - 1])
        below = below + jnp.where(under, value, zero)
        above = above + jnp.where(under, zero, value)
    layers = [
        moment_ref[z, l * channels : (l + 1) * channels, :] for z in range(zcells) for l in range(2)
    ]
    down = []
    for layer in layers:
        below = decay * below + layer
        down.append(below)
    up = [above]
    for layer in layers[:0:-1]:
        above = decay * (above + layer)
        up.append(above)
    up = up[::-1]
    row_atoms = xcells * slots
    for z in range(zcells):
        lanes = slice(z * row_atoms, (z + 1) * row_atoms)
        rows = []
        for l in range(2):
            field = down[2 * z + l] + up[2 * z + l]
            cosine = field[:, :WAVES] * weight
            sine = field[:, WAVES:] * weight
            rows.append(jnp.concatenate([cosine, sine], axis=1))
            rows.append(jnp.concatenate([wave_x * sine, -wave_x * cosine], axis=1))
            rows.append(jnp.concatenate([wave_y * sine, -wave_y * cosine], axis=1))
        panel = jnp.concatenate([row.astype(bf16) for row in rows], axis=0)
        evaluated = nn_dot(panel, phase_ref[:, lanes])
        sub = msg_ref[channels : channels + 16, lanes].astype(f32)[6:7]
        chosen = jnp.where(sub == 0.0, evaluated[: 3 * channels], evaluated[3 * channels :])
        charges = msg_ref[0:channels, lanes].astype(f32)
        long_energy = 0.5 * jnp.sum(charges * chosen[:channels], axis=0, keepdims=True)
        force_x = -jnp.sum(charges * chosen[channels : 2 * channels], axis=0, keepdims=True)
        force_y = -jnp.sum(charges * chosen[2 * channels :], axis=0, keepdims=True)
        energy = short[:, lanes] + long_energy
        for x in range(xcells):
            cell = z * xcells + x
            piece = slice(x * slots, (x + 1) * slots)
            energy_ref[cell : cell + 1, :] = energy[:, piece]
            force_ref[0, cell : cell + 1, :] = force_x[:, piece]
            force_ref[1, cell : cell + 1, :] = force_y[:, piece]


def vmem():
    return pl.BlockSpec(memory_space=pltpu.VMEM)


def hbm():
    return pl.BlockSpec(memory_space=pltpu.HBM)


def fetching(body, count):
    def kernel(*refs):
        copies, sems = refs[-count - 1 : -1], refs[-1]
        moves = [
            pltpu.make_async_copy(refs[i], copies[i], sems.at[i]) for i in range(count)
        ]
        for move in moves:
            move.start()
        for move in moves:
            move.wait()
        body(*copies, *refs[count : -count - 1])

    kernel.__name__ = body.__name__
    return kernel


def held(arrays):
    return [pltpu.with_memory_space_constraint(a, pltpu.HBM) for a in arrays]


def fetch_scratch(arrays):
    return [pltpu.VMEM(a.shape, a.dtype) for a in arrays] + [
        pltpu.SemaphoreType.DMA((len(arrays),))
    ]


def shards(
    features,
    species,
    sublayer,
    offsets,
    neighbours,
    neighbour_count,
    distances,
    species_table,
    charge_weight,
    radial_in,
    radial_out,
    update_in,
    update_out,
    energy_weight,
):
    zcells, xcells, slots, width = features.shape
    channels = charge_weight.shape[1]
    listed = neighbours.shape[3]
    cells = zcells * xcells
    atoms = cells * slots
    strips = lax.axis_size("xy")
    slabs = lax.axis_size("gz")
    width_x = cell_width * (xcells * strips)

    def shape(dims, kind):
        return jax.ShapeDtypeStruct(dims, kind)

    def partial(body, *static):
        def kernel(*refs):
            body(*static, *refs)

        kernel.__name__ = body.__name__
        return kernel

    def grant(mebibytes):
        return pltpu.CompilerParams(vmem_limit_bytes=mebibytes * 1024 * 1024)

    def cost(flops, data):
        return pl.CostEstimate(flops=flops, bytes_accessed=data, transcendentals=0)

    inputs = (
        features.reshape(atoms, width),
        species.reshape(cells, slots),
        sublayer.reshape(cells, slots),
        offsets.reshape(2, cells, slots),
        species_table,
        charge_weight.T,
    )
    hidden, message, even_message, odd_message = pl.pallas_call(
        fetching(partial(start_kernel, zcells, xcells, slots), len(inputs)),
        out_shape=(
            shape((atoms, width), bf16),
            shape((channels + 16, atoms), bf16),
            shape((channels + 32, atoms), bf16),
            shape((channels + 32, atoms), bf16),
        ),
        in_specs=[hbm()] * len(inputs),
        out_specs=(vmem(),) * 4,
        scratch_shapes=fetch_scratch(inputs),
        compiler_params=grant(6),
    )(*held(inputs))

    paths = routes(strips)
    payloads = [even_message, odd_message] + [message] * (len(paths) - 2)
    messages = [lax.ppermute(p, "xy", path) for p, path in zip(payloads, paths)]

    rows = listed * slots // 128
    chunks = rows // 2
    basis, hidden_width = radial_in.shape
    inputs = (
        neighbours.reshape(cells, slots, listed),
        distances.reshape(cells, slots, listed),
        neighbour_count.reshape(cells, slots),
        radial_in,
    )
    phases, own_moments, table, weight, filters = pl.pallas_call(
        partial(own_kernel, zcells, channels, width_x, slots),
        out_shape=(
            shape((2 * WAVES, atoms), bf16),
            shape((zcells, 2 * channels, 2 * WAVES), f32),
            shape((cells, rows, 128), jnp.int32),
            shape((cells, rows, 128), f32),
            shape((cells, hidden_width, rows * 128), bf16),
        ),
        in_specs=[hbm()] * len(inputs) + [vmem()],
        out_specs=(vmem(),) * 5,
        scratch_shapes=[pltpu.VMEM(a.shape, a.dtype) for a in inputs]
        + [
            pltpu.VMEM((2, basis, rows * 128), bf16),
            pltpu.VMEM((2, basis, rows * 128), bf16),
            pltpu.SemaphoreType.DMA((len(inputs),)),
        ],
        compiler_params=grant(10),
        cost_estimate=cost(6_000_000_000, 4_000_000),
    )(*held(inputs), message)

    wide = ((xcells + 2) * slots, width)
    first, second, own_rows = pl.pallas_call(
        partial(extend_kernel, zcells, xcells, slots, channels),
        out_shape=(shape(wide, bf16), shape(wide, bf16), shape((zcells,) + wide, bf16)),
        in_specs=[vmem()] * 3,
        out_specs=(vmem(),) * 3,
        compiler_params=grant(4),
    )(hidden, messages[0], messages[1])
    paths = routes(slabs)
    first = lax.ppermute(first, "gz", paths[0])
    second = lax.ppermute(second, "gz", paths[1])

    slab = pl.pallas_call(
        partial(slab_kernel, zcells, channels, width_x, slabs, len(messages)),
        out_shape=(shape((zcells, 2 * channels, 2 * WAVES), f32),)
        + (shape((channels, 2 * WAVES), f32),) * (slabs - 1),
        in_specs=[vmem()] * (1 + len(messages)),
        out_specs=(vmem(),) * slabs,
        scratch_shapes=[pltpu.VMEM((2 * WAVES, atoms // zcells), bf16)],
        compiler_params=grant(8),
        cost_estimate=cost(8_000_000_000, 2_000_000),
    )(own_moments, *messages)
    sums = [lax.ppermute(part, "gz", path) for part, path in zip(slab[1:], paths)]

    region = 9 * slots // 2
    aggregate = pl.pallas_call(
        partial(edge_kernel, zcells, xcells, slots, slabs),
        out_shape=shape((atoms // 128, width, 128), f32),
        in_specs=[vmem()] * 7,
        out_specs=vmem(),
        scratch_shapes=[pltpu.VMEM((zcells + 2,) + wide, bf16)]
        + [pltpu.VMEM((2 * width, region), bf16)] * 2
        + [pltpu.VMEM((chunks, region, 256), bf16)] * 2
        + [pltpu.VMEM((chunks, 2 * width, 256), f32)] * 2
        + [pltpu.VMEM((chunks, width, 256), f32)] * 2,
        compiler_params=grant(12),
        cost_estimate=cost(12_000_000_000, 4_000_000),
    )(first, second, own_rows, table, weight, filters, radial_out)

    features_out, energy, forces = pl.pallas_call(
        partial(field_kernel, zcells, xcells, slots, channels, width_x, slabs),
        out_shape=(
            shape((atoms, width), bf16),
            shape((cells, slots), f32),
            shape((2, cells, slots), f32),
        ),
        in_specs=[vmem()] * (8 + len(sums)),
        out_specs=(vmem(),) * 3,
        compiler_params=grant(8),
        cost_estimate=cost(3_000_000_000, 3_000_000),
    )(
        message,
        phases,
        slab[0],
        hidden,
        aggregate,
        update_in,
        update_out,
        energy_weight.reshape(1, width),
        *sums,
    )

    return (
        features_out.reshape(features.shape),
        energy.reshape(species.shape),
        forces.reshape(offsets.shape),
    )


def solution(mesh):
    in_specs = (
        P(("groups", "gz"), "xy", None, None),
        P(("groups", "gz"), "xy", None),
        P(("groups", "gz"), "xy", None),
        P(None, ("groups", "gz"), "xy", None),
        P(("groups", "gz"), "xy", None, None),
        P(("groups", "gz"), "xy", None),
        P(("groups", "gz"), "xy", None, None),
        P(),
        P(),
        P(),
        P(),
        P(),
        P(),
        P(),
    )
    out_specs = (
        P(("groups", "gz"), "xy", None, None),
        P(("groups", "gz"), "xy", None),
        P(None, ("groups", "gz"), "xy", None),
    )
    return jax.shard_map(shards, mesh=mesh, in_specs=in_specs, out_specs=out_specs, check_vma=False)
```

```python
import math

import jax
import jax.numpy as jnp
from jax import lax
from jax.experimental import pallas as pl
from jax.experimental.pallas import tpu as pltpu
from jax.sharding import PartitionSpec as P

KX = 128
KY = 8

cell_width = 11.0
layer_depth = 5.5
screening = 0.025
smearing = 1.0
coupling = 0.25
cutoff = 8.0
basis_width = 1.0

HALF_X = KX // 2
HALF_Y = KY // 2
WAVES = 640

f32 = jnp.float32
bf16 = jnp.bfloat16

SIN_TERMS = (9.99999996e-01, -1.66666580e-01, 8.33305062e-03, -1.98090464e-04, 2.60516628e-06)
COS_TERMS = (9.99999953e-01, -4.99999051e-01, 4.16635789e-02, -1.38536669e-03, 2.31531742e-05)


def nt_dot(a, b):
    return lax.dot_general(a, b, (((1,), (1,)), ((), ())), preferred_element_type=f32)


def nn_dot(a, b):
    return lax.dot_general(a, b, (((1,), (0,)), ((), ())), preferred_element_type=f32)


def tn_dot(a, b):
    return lax.dot_general(a, b, (((0,), (0,)), ((), ())), preferred_element_type=f32)


def polynomial(z, terms):
    value = jnp.full_like(z, terms[-1])
    for term in terms[-2::-1]:
        value = value * z + term
    return value


def cos_sin(angle):
    turns = jnp.floor(angle * (1.0 / (2.0 * math.pi)) + 0.5)
    head = 6.28125
    rest = (angle - turns * head) - turns * (2.0 * math.pi - head)
    half = rest * 0.5
    z = half * half
    s = half * polynomial(z, SIN_TERMS)
    c = polynomial(z, COS_TERMS)
    return 1.0 - 2.0 * (s * s), 2.0 * (s * c)


def wave_row(width_x):
    lane = lax.broadcasted_iota(jnp.int32, (1, WAVES), 1)
    block = lane // HALF_X
    place = lane % HALF_X
    edge = block == 2 * HALF_Y + 1
    minus = (block > 0) & (block % 2 == 0)
    step_x = jnp.where(
        edge, jnp.where(place <= HALF_Y, HALF_X, -HALF_X), jnp.where(minus, -place, place)
    )
    step_y = jnp.where(
        edge, jnp.where(place <= HALF_Y, place, place - HALF_Y), (block + 1) // 2
    )
    inner = (place > 0) | ((block > 0) & (step_y < HALF_Y))
    twice = inner & ((step_y < HALF_Y))
    plain = jnp.where(minus & (place == 0), 0, jnp.where(twice, 2, 1))
    count = jnp.where(edge, jnp.where(place < 2 * HALF_Y, 1, 0), plain).astype(f32)
    wave_x = 2.0 * math.pi / width_x * step_x.astype(f32)
    wave_y = 2.0 * math.pi / cell_width * step_y.astype(f32)
    square = wave_x * wave_x + wave_y * wave_y
    screened = jnp.sqrt(square + screening * screening)
    weight = (
        coupling
        * (2.0 * math.pi / (width_x * cell_width))
        * jnp.exp(-0.5 * smearing * smearing * square)
        / screened
    )
    return wave_x, wave_y, screened, weight * count


def twin(row):
    return jnp.concatenate([row, row], axis=1)


def store_phases(out_ref, lanes, coord_x, coord_y, width_x):
    count = coord_x.shape[1]
    row = lax.broadcasted_iota(jnp.int32, (8, count), 0)
    step_y = jnp.where(row <= HALF_Y, row, row - HALF_Y).astype(f32)
    unit_x = 2.0 * math.pi / width_x * row.astype(f32)
    cosine, sine = cos_sin(
        jnp.concatenate(
            [
                unit_x * coord_x,
                (8.0 * unit_x) * coord_x,
                (2.0 * math.pi / cell_width * step_y) * coord_y,
            ],
            axis=0,
        )
    )
    fine_c, fine_s = cosine[:8], sine[:8]
    cos_y, sin_y = cosine[16:], sine[16:]
    main_c, main_s = [fine_c], [fine_s]
    for h in range(1, HALF_X // 8):
        hc, hs = cosine[8 + h : 9 + h], sine[8 + h : 9 + h]
        main_c.append(hc * fine_c - hs * fine_s)
        main_s.append(hs * fine_c + hc * fine_s)
    last_c, last_s = cosine[7 + HALF_X // 8 : 8 + HALF_X // 8], sine[7 + HALF_X // 8 : 8 + HALF_X // 8]
    edge_c = last_c * cosine[9:10] - last_s * sine[9:10]
    edge_s = last_s * cosine[9:10] + last_c * sine[9:10]
    main_c, main_s = jnp.concatenate(main_c, axis=0), jnp.concatenate(main_s, axis=0)

    def put(block, cosine, sine):
        rows = cosine.shape[0]
        out_ref[block * HALF_X : block * HALF_X + rows, lanes] = cosine.astype(bf16)
        out_ref[WAVES + block * HALF_X : WAVES + block * HALF_X + rows, lanes] = sine.astype(bf16)

    put(0, main_c, main_s)
    for b in range(1, HALF_Y + 1):
        cb, sb = cos_y[b : b + 1], sin_y[b : b + 1]
        cc, ss, sc, cs = main_c * cb, main_s * sb, main_s * cb, main_c * sb
        put(2 * b - 1, cc - ss, sc + cs)
        put(2 * b, cc + ss, cs - sc)
    edge_s = jnp.where(row <= HALF_Y, edge_s, -edge_s)
    blank = jnp.zeros((HALF_X - 2 * HALF_Y, count), f32)
    put(
        2 * HALF_Y + 1,
        jnp.concatenate([edge_c * cos_y - edge_s * sin_y, blank], axis=0),
        jnp.concatenate([edge_s * cos_y + edge_c * sin_y, blank], axis=0),
    )


def layer_charges(charges, sub):
    return jnp.concatenate(
        [
            jnp.where(sub == 0.0, charges, 0.0).astype(bf16),
            jnp.where(sub == 1.0, charges, 0.0).astype(bf16),
        ],
        axis=0,
    )


def lane_rows(read, cells, slots):
    per = 128 // slots
    cat = jnp.concatenate(
        [read(pl.ds(j, cells // per, stride=per)) for j in range(per)], axis=1
    )
    return jnp.concatenate([cat[q : q + 1] for q in range(cells // per)], axis=1)


def three_parts(value):
    head = value.astype(bf16).astype(f32)
    middle = (value - head).astype(bf16).astype(f32)
    return [head, middle, (value - head) - middle]


def start_kernel(zcells, xcells, slots, feat_ref, spec_ref, sub_ref, off_ref, table_ref,
                 cw_ref, hid_ref, msg_ref, even_ref, odd_ref):
    cells = zcells * xcells
    atoms = cells * slots
    kinds = table_ref.shape[0]
    spec = lane_rows(lambda rows: spec_ref[rows, :], cells, slots)
    onehot = (lax.broadcasted_iota(jnp.int32, (kinds, atoms), 0) == spec).astype(f32)
    embedded = tn_dot(onehot, table_ref[...].astype(f32))
    hidden = (feat_ref[...].astype(f32) + embedded).astype(bf16)
    hid_ref[...] = hidden
    charges = nt_dot(cw_ref[...], hidden).astype(bf16)
    channels = charges.shape[0]
    sub = lane_rows(lambda rows: sub_ref[rows, :], cells, slots).astype(f32)
    lane_cell = lax.broadcasted_iota(jnp.int32, (1, atoms), 1) // slots % xcells
    cell_x = (lax.axis_index("xy") * xcells + lane_cell).astype(f32)
    coord_x = cell_width * cell_x + lane_rows(lambda rows: off_ref[0, rows, :], cells, slots)
    coord_y = lane_rows(lambda rows: off_ref[1, rows, :], cells, slots)
    extra = jnp.concatenate(
        three_parts(coord_x)
        + three_parts(coord_y)
        + [sub, jnp.zeros((1, atoms), f32)],
        axis=0,
    ).astype(bf16)
    msg_ref[0:channels, :] = charges
    msg_ref[channels : channels + 8, :] = extra
    even = lax.axis_index("xy") % 2 == 0
    right = xcells - 1
    for ref, column in ((even_ref, jnp.where(even, right, 0)), (odd_ref, jnp.where(even, 0, right))):
        ref[0:channels, :] = charges
        ref[channels + 16 : channels + 24, :] = extra
        for z in range(zcells):
            for h in range(slots // 16):
                begin = pl.multiple_of((z * xcells + column) * slots + 16 * h, 16)
                lane = (z * (slots // 16) + h) * 128
                ref[channels : channels + 16, lane : lane + 128] = hid_ref[
                    pl.ds(begin, 16), :
                ]


def read_atoms(msg_ref, channels, lanes):
    charges = msg_ref[0:channels, lanes].astype(f32)
    extra = msg_ref[msg_ref.shape[0] - 8 :, lanes].astype(f32)
    coord_x = (extra[0:1] + extra[1:2]) + extra[2:3]
    coord_y = (extra[3:4] + extra[4:5]) + extra[5:6]
    return charges, coord_x, coord_y, extra[6:7]


def pair(table, q):
    return jnp.concatenate([table[2 * q : 2 * q + 1], table[2 * q + 1 : 2 * q + 2]], axis=1)


def own_kernel(zcells, channels, width_x, slots, near_ref, dist_ref, count_ref, rin_ref, rout_ref,
               msg_ref, phase_ref, moment_ref, table_ref, filter_ref, weight_ref, rad_ref,
               layer_a, layer_b):
    row_atoms = msg_ref.shape[1] // zcells
    for z in range(zcells):
        lanes = slice(z * row_atoms, (z + 1) * row_atoms)
        charges, coord_x, coord_y, sub = read_atoms(msg_ref, channels, lanes)
        store_phases(phase_ref, lanes, coord_x, coord_y, width_x)
        moment_ref[z] = nt_dot(layer_charges(charges, sub), phase_ref[:, lanes])

    cells, _, listed = near_ref.shape
    basis = rin_ref.shape[0]
    groups = 128 // slots
    rows = listed // groups
    rin_t = (0.5 * rin_ref[...].astype(f32)).T.astype(bf16)
    rout_t = rout_ref[...].astype(f32).T.astype(bf16)
    centre = (
        cutoff * lax.broadcasted_iota(jnp.int32, (basis, 128), 0).astype(f32) / (basis - 1)
    )
    lane8 = lax.broadcasted_iota(jnp.int32, (rows, 128), 1)
    slot8 = lane8 % slots
    listed8 = (lane8 // slots) * rows + lax.broadcasted_iota(jnp.int32, (rows, 128), 0)

    def edge_rows(block):
        turned = block.T
        return jnp.concatenate(
            [turned[g * rows : (g + 1) * rows] for g in range(groups)], axis=1
        )

    def spread(cell, slot):
        near = edge_rows(near_ref[cell].astype(f32)).astype(jnp.int32)
        dist = edge_rows(dist_ref[cell])
        count = jnp.concatenate([count_ref[pl.ds(cell, 1), :]] * groups, axis=1)
        usable = (listed8 < count) & jnp.logical_not(near == 4 * slots + slot8)
        part = 1.0 - jnp.square(dist * (1.0 / cutoff))
        table_ref[cell] = near
        weight_ref[cell] = jnp.where(usable, part * part, 0.0)
        for q in range(rows):
            gap = (dist[q : q + 1] - centre) / basis_width
            rad_ref[slot, :, 128 * q : 128 * q + 128] = jnp.exp(-(gap * gap)).astype(bf16)

    def first_layer(slot, layer_ref):
        for q in range(0, rows * 128, 256):
            half = nn_dot(rin_t, rad_ref[slot, :, q : q + 256])
            layer_ref[slot, :, q : q + 256] = (half + half * jnp.tanh(half)).astype(bf16)

    def second_layer(cell, slot, layer_ref):
        weight = weight_ref[cell]
        for q in range(rows // 2):
            wide = nn_dot(rout_t, layer_ref[slot, :, 256 * q : 256 * q + 256])
            filter_ref[cell, q] = pair(weight, q) * wide

    def advance(cell, done_ref, next_ref):
        for slot in range(2):
            first_layer(slot, next_ref)
        for slot in range(2):
            second_layer(cell + slot, slot, done_ref)
        for slot in range(2):
            spread(jnp.minimum(cell + 4 + slot, cells - 1), slot)

    for slot in range(2):
        spread(slot, slot)
    for slot in range(2):
        first_layer(slot, layer_a)
    for slot in range(2):
        spread(2 + slot, slot)

    def four_cells(turn, carry):
        advance(4 * turn, layer_a, layer_b)
        advance(4 * turn + 2, layer_b, layer_a)
        return carry

    lax.fori_loop(0, cells // 4, four_cells, 0)


def targets(place, count):
    even = place % 2 == 0
    above, below = (place + 1) % count, (place + count - 1) % count
    return [jnp.where(even, above, below), jnp.where(even, below, above)] + [
        (place + shift) % count for shift in range(2, count - 1)
    ]


def routes(count):
    even = [(i, i + 1 if i % 2 == 0 else i - 1) for i in range(count)]
    odd = [(i, (i + 1) % count if i % 2 == 1 else (i - 1) % count) for i in range(count)]
    return [even, odd] + [
        [(i, (i + shift) % count) for i in range(count)] for shift in range(2, count - 1)
    ]


def slab_kernel(zcells, channels, width_x, slabs, others, own_ref, *refs):
    msg_refs = refs[:others]
    moment_ref = refs[others]
    send_refs = refs[others + 1 : others + slabs]
    scratch = refs[others + slabs]
    row_atoms = msg_refs[0].shape[1] // zcells
    for z in range(zcells):
        total = own_ref[z]
        for ref in msg_refs:
            lanes = slice(z * row_atoms, (z + 1) * row_atoms)
            charges, coord_x, coord_y, sub = read_atoms(ref, channels, lanes)
            store_phases(scratch, slice(0, row_atoms), coord_x, coord_y, width_x)
            total = total + nt_dot(layer_charges(charges, sub), scratch[...])
        moment_ref[z] = total
    screened = wave_row(width_x)[2]
    decay = twin(jnp.exp(-screened * layer_depth))
    layers = [
        moment_ref[z, l * channels : (l + 1) * channels, :] for z in range(zcells) for l in range(2)
    ]
    top = layers[0]
    for layer in layers[1:]:
        top = decay * top + layer
    bottom = decay * layers[-1]
    for layer in layers[-2::-1]:
        bottom = decay * (bottom + layer)
    place = lax.axis_index("gz")
    for target, ref in zip(targets(place, slabs), send_refs):
        ref[...] = jnp.where(target > place, top, bottom)


def sides(even_ref, odd_ref, rows, lanes):
    first, second = even_ref[rows, lanes], odd_ref[rows, lanes]
    even = lax.axis_index("xy") % 2 == 0
    return jnp.where(even, second, first), jnp.where(even, first, second)


def fill_row(ref, z, xcells, slots, channels, hid_ref, even_ref, odd_ref):
    count = xcells * slots
    ref[slots : slots + count, :] = hid_ref[z * count : (z + 1) * count, :]
    for h in range(slots // 16):
        lane = (z * (slots // 16) + h) * 128
        left, right = sides(
            even_ref, odd_ref, slice(channels, channels + 16), slice(lane, lane + 128)
        )
        ref[16 * h : 16 * h + 16, :] = left
        begin = slots + count + 16 * h
        ref[begin : begin + 16, :] = right


def extend_kernel(zcells, xcells, slots, channels, hid_ref, even_ref, odd_ref, first_ref,
                  second_ref, ext_ref):
    for z in range(zcells):
        fill_row(ext_ref.at[z], z, xcells, slots, channels, hid_ref, even_ref, odd_ref)
    even = lax.axis_index("gz") % 2 == 0
    first_ref[...] = ext_ref[jnp.where(even, zcells - 1, 0)]
    second_ref[...] = ext_ref[jnp.where(even, 0, zcells - 1)]


def edge_kernel(zcells, xcells, slots, slabs, first_ref, second_ref, own_ref, table_ref, filter_ref,
                agg_ref, ext_ref, rows_a, rows_b, hot_a, hot_b, both_a, both_b):
    features = own_ref.shape[2]
    cells = zcells * xcells
    place = lax.axis_index("gz")
    even = place % 2 == 0
    first, second = first_ref[...], second_ref[...]
    blank = jnp.zeros_like(first)
    ext_ref[0] = jnp.where(place > 0, jnp.where(even, second, first), blank)
    ext_ref[zcells + 1] = jnp.where(place < slabs - 1, jnp.where(even, first, second), blank)
    ext_ref[1 : zcells + 1] = own_ref[...]
    groups = 128 // slots
    chunks = table_ref.shape[1] // 2
    region = 9 * slots // 2
    row_id = lax.broadcasted_iota(jnp.int32, (16, 256), 0).astype(jnp.int16)
    one, zero = jnp.ones((16, 256), bf16), jnp.zeros((16, 256), bf16)
    group_lane = lax.broadcasted_iota(jnp.int32, (features, 128), 1) // slots

    def make_hot(cell, hot_ref, rows_ref):
        near = table_ref[cell]
        index = jnp.where(near >= region, near - region, near)
        for q in range(chunks):
            column = jnp.broadcast_to(pair(index, q), (16, 256)).astype(jnp.int16)
            for r in range(0, region, 16):
                hot_ref[q, r : r + 16, :] = jnp.where(column == row_id + r, one, zero)
        z = cell // xcells
        begin = pl.multiple_of(cell % xcells * slots, slots)
        rows = jnp.concatenate(
            [ext_ref[z + dz, pl.ds(begin, 3 * slots), :] for dz in range(3)], axis=0
        )
        rows_ref[:features] = rows[:region].astype(f32).T.astype(bf16)
        rows_ref[features:] = rows[region:].astype(f32).T.astype(bf16)

    def multiply(hot_ref, rows_ref, both_ref):
        rows_t = rows_ref[...]
        for q in range(chunks):
            both_ref[q] = nn_dot(rows_t, hot_ref[q])

    def gather_up(cell, both_ref):
        near = table_ref[cell]
        total = jnp.zeros((features, 128), f32)
        for q in range(chunks):
            upper = pair(near, q) >= region
            picked = jnp.where(upper, both_ref[q, features:], both_ref[q, :features])
            product = filter_ref[cell, q] * picked
            total = total + (product[:, :128] + product[:, 128:])
        shift = 64
        while shift >= slots:
            total = total + pltpu.roll(total, shift, 1)
            shift //= 2
        step = cell // groups
        agg_ref[step] = jnp.where(group_lane == cell % groups, total, agg_ref[step])

    make_hot(0, hot_a, rows_a)

    def eight_cells(turn, carry):
        for step in range(4):
            cell = 8 * turn + 2 * step
            multiply(hot_a, rows_a, both_a)
            make_hot(cell + 1, hot_b, rows_b)
            gather_up(jnp.maximum(cell - 1, 0), both_b)
            multiply(hot_b, rows_b, both_b)
            make_hot(jnp.minimum(cell + 2, cells - 1), hot_a, rows_a)
            gather_up(cell, both_a)
        return carry

    lax.fori_loop(0, cells // 8, eight_cells, 0)
    gather_up(cells - 1, both_b)


def field_kernel(zcells, xcells, slots, channels, width_x, slabs, msg_ref, phase_ref, moment_ref,
                 hid_ref, agg_ref, uin_ref, uout_ref, ew_ref, *refs):
    sums = [ref[...] for ref in refs[: slabs - 1]]
    out_ref, energy_ref, force_ref = refs[slabs - 1 :]

    aggregate = jnp.concatenate(
        [agg_ref[step].astype(bf16) for step in range(agg_ref.shape[0])], axis=1
    )
    uin_t = (0.5 * uin_ref[...].astype(f32)).T.astype(bf16)
    uout_t = uout_ref[...].astype(f32).T.astype(bf16)
    half = nn_dot(uin_t, aggregate)
    update = nn_dot(uout_t, (half + half * jnp.tanh(half)).astype(bf16))
    readout = ew_ref[...]
    energy_column = jnp.broadcast_to(readout.astype(f32), (8, readout.shape[1])).T[:, :1]
    short = jnp.sum(update * energy_column, axis=0, keepdims=True) + nt_dot(
        jnp.broadcast_to(readout, (16, readout.shape[1])), hid_ref[...]
    )[:1]
    out_ref[...] = (hid_ref[...].astype(f32) + update.T).astype(bf16)

    wave_x, wave_y, screened, weight = wave_row(width_x)
    decay = twin(jnp.exp(-screened * layer_depth))
    span = decay
    for _ in range(2 * zcells - 1):
        span = span * decay
    spans = [jnp.ones_like(span)]
    for _ in range(slabs - 2):
        spans.append(spans[-1] * span)
    place = lax.axis_index("gz")
    even = place % 2 == 0
    inner = jnp.where(even, place > 0, place < slabs - 1)
    near, other = sums[0], sums[1]
    other = jnp.where(inner, other, other * spans[-1])
    other_below = jnp.where(even, place > 0, place == slabs - 1)
    zero = jnp.zeros_like(near)
    below = jnp.where(even, zero, near) + jnp.where(other_below, other, zero)
    above = jnp.where(even, near, zero) + jnp.where(other_below, zero, other)
    for shift, value in enumerate(sums[2:], start=2):
        under = place >= shift
        value = value * jnp.where(under, spans[shift - 1], spans[slabs - shift - 1])
        below = below + jnp.where(under, value, zero)
        above = above + jnp.where(under, zero, value)
    layers = [
        moment_ref[z, l * channels : (l + 1) * channels, :] for z in range(zcells) for l in range(2)
    ]
    down = []
    for layer in layers:
        below = decay * below + layer
        down.append(below)
    up = [above]
    for layer in layers[:0:-1]:
        above = decay * (above + layer)
        up.append(above)
    up = up[::-1]
    row_atoms = xcells * slots
    for z in range(zcells):
        lanes = slice(z * row_atoms, (z + 1) * row_atoms)
        rows = []
        for l in range(2):
            field = down[2 * z + l] + up[2 * z + l]
            cosine = field[:, :WAVES] * weight
            sine = field[:, WAVES:] * weight
            rows.append(jnp.concatenate([cosine, sine], axis=1))
            rows.append(jnp.concatenate([wave_x * sine, -wave_x * cosine], axis=1))
            rows.append(jnp.concatenate([wave_y * sine, -wave_y * cosine], axis=1))
        panel = jnp.concatenate([row.astype(bf16) for row in rows], axis=0)
        evaluated = nn_dot(panel, phase_ref[:, lanes])
        sub = msg_ref[channels : channels + 8, lanes].astype(f32)[6:7]
        chosen = jnp.where(sub == 0.0, evaluated[: 3 * channels], evaluated[3 * channels :])
        charges = msg_ref[0:channels, lanes].astype(f32)
        long_energy = 0.5 * jnp.sum(charges * chosen[:channels], axis=0, keepdims=True)
        force_x = -jnp.sum(charges * chosen[channels : 2 * channels], axis=0, keepdims=True)
        force_y = -jnp.sum(charges * chosen[2 * channels :], axis=0, keepdims=True)
        energy = short[:, lanes] + long_energy
        for x in range(xcells):
            cell = z * xcells + x
            piece = slice(x * slots, (x + 1) * slots)
            energy_ref[cell : cell + 1, :] = energy[:, piece]
            force_ref[0, cell : cell + 1, :] = force_x[:, piece]
            force_ref[1, cell : cell + 1, :] = force_y[:, piece]


def vmem():
    return pl.BlockSpec(memory_space=pltpu.VMEM)


def hbm():
    return pl.BlockSpec(memory_space=pltpu.HBM)


def fetching(body, count, through):
    def kernel(*refs):
        copies, sems = refs[-count - 1 : -1], refs[-1]
        given, rest = refs[: count + through], refs[count + through : -count - 1]
        kept = rest[len(rest) - through :]
        moves = [
            pltpu.make_async_copy(source, target, sems.at[i])
            for i, (source, target) in enumerate(zip(given, copies + kept))
        ]
        for move in moves:
            move.start()
        for move in moves[:count]:
            move.wait()
        body(*copies, *rest[: len(rest) - through])
        for move in moves[count:]:
            move.wait()

    kernel.__name__ = body.__name__
    return kernel


def held(arrays):
    return [pltpu.with_memory_space_constraint(a, pltpu.HBM) for a in arrays]


def shards(
    features,
    species,
    sublayer,
    offsets,
    neighbours,
    neighbour_count,
    distances,
    species_table,
    charge_weight,
    radial_in,
    radial_out,
    update_in,
    update_out,
    energy_weight,
):
    zcells, xcells, slots, width = features.shape
    channels = charge_weight.shape[1]
    listed = neighbours.shape[3]
    cells = zcells * xcells
    atoms = cells * slots
    strips = lax.axis_size("xy")
    slabs = lax.axis_size("gz")
    width_x = cell_width * (xcells * strips)

    def shape(dims, kind):
        return jax.ShapeDtypeStruct(dims, kind)

    def partial(body, *static):
        def kernel(*refs):
            body(*static, *refs)

        kernel.__name__ = body.__name__
        return kernel

    def grant(mebibytes):
        return pltpu.CompilerParams(vmem_limit_bytes=mebibytes * 1024 * 1024)

    def cost(flops, data):
        return pl.CostEstimate(flops=flops, bytes_accessed=data, transcendentals=0)

    inputs = (
        features.reshape(atoms, width),
        species.reshape(cells, slots),
        sublayer.reshape(cells, slots),
        offsets.reshape(2, cells, slots),
        species_table,
        charge_weight.T,
    )
    through = (
        neighbours.reshape(cells, slots, listed),
        distances.reshape(cells, slots, listed),
        neighbour_count.reshape(cells, slots),
        radial_in,
        radial_out,
    )
    hidden, message, even_message, odd_message, *lists = pl.pallas_call(
        fetching(partial(start_kernel, zcells, xcells, slots), len(inputs), len(through)),
        out_shape=(
            shape((atoms, width), bf16),
            shape((channels + 8, atoms), bf16),
            shape((channels + 24, atoms), bf16),
            shape((channels + 24, atoms), bf16),
        )
        + tuple(shape(a.shape, a.dtype) for a in through),
        in_specs=[hbm()] * (len(inputs) + len(through)),
        out_specs=(vmem(),) * (4 + len(through)),
        scratch_shapes=[pltpu.VMEM(a.shape, a.dtype) for a in inputs]
        + [pltpu.SemaphoreType.DMA((len(inputs) + len(through),))],
        compiler_params=grant(6),
    )(*held(inputs + through))

    paths = routes(strips)
    payloads = [even_message, odd_message] + [message] * (len(paths) - 2)
    messages = [lax.ppermute(p, "xy", path) for p, path in zip(payloads, paths)]

    rows = listed * slots // 128
    chunks = rows // 2
    basis, hidden_width = radial_in.shape
    phases, own_moments, table, filters = pl.pallas_call(
        partial(own_kernel, zcells, channels, width_x, slots),
        out_shape=(
            shape((2 * WAVES, atoms), bf16),
            shape((zcells, 2 * channels, 2 * WAVES), f32),
            shape((cells, rows, 128), jnp.int32),
            shape((cells, chunks, width, 256), f32),
        ),
        in_specs=[vmem()] * (len(lists) + 1),
        out_specs=(vmem(),) * 4,
        scratch_shapes=[
            pltpu.VMEM((cells, rows, 128), f32),
            pltpu.VMEM((2, basis, rows * 128), bf16),
            pltpu.VMEM((2, hidden_width, rows * 128), bf16),
            pltpu.VMEM((2, hidden_width, rows * 128), bf16),
        ],
        compiler_params=grant(16),
        cost_estimate=cost(6_000_000_000, 4_000_000),
    )(*lists, message)
    wide = ((xcells + 2) * slots, width)
    first, second, own_rows = pl.pallas_call(
        partial(extend_kernel, zcells, xcells, slots, channels),
        out_shape=(shape(wide, bf16), shape(wide, bf16), shape((zcells,) + wide, bf16)),
        in_specs=[vmem()] * 3,
        out_specs=(vmem(),) * 3,
        compiler_params=grant(4),
    )(hidden, messages[0], messages[1])
    paths = routes(slabs)
    first = lax.ppermute(first, "gz", paths[0])
    second = lax.ppermute(second, "gz", paths[1])

    slab = pl.pallas_call(
        partial(slab_kernel, zcells, channels, width_x, slabs, len(messages)),
        out_shape=(shape((zcells, 2 * channels, 2 * WAVES), f32),)
        + (shape((channels, 2 * WAVES), f32),) * (slabs - 1),
        in_specs=[vmem()] * (1 + len(messages)),
        out_specs=(vmem(),) * slabs,
        scratch_shapes=[pltpu.VMEM((2 * WAVES, atoms // zcells), bf16)],
        compiler_params=grant(8),
        cost_estimate=cost(8_000_000_000, 2_000_000),
    )(own_moments, *messages)
    sums = [lax.ppermute(part, "gz", path) for part, path in zip(slab[1:], paths)]

    region = 9 * slots // 2
    aggregate = pl.pallas_call(
        partial(edge_kernel, zcells, xcells, slots, slabs),
        out_shape=shape((atoms // 128, width, 128), f32),
        in_specs=[vmem()] * 5,
        out_specs=vmem(),
        scratch_shapes=[pltpu.VMEM((zcells + 2,) + wide, bf16)]
        + [pltpu.VMEM((2 * width, region), bf16)] * 2
        + [pltpu.VMEM((chunks, region, 256), bf16)] * 2
        + [pltpu.VMEM((chunks, 2 * width, 256), f32)] * 2,
        compiler_params=grant(16),
        cost_estimate=cost(12_000_000_000, 4_000_000),
    )(first, second, own_rows, table, filters)

    features_out, energy, forces = pl.pallas_call(
        partial(field_kernel, zcells, xcells, slots, channels, width_x, slabs),
        out_shape=(
            shape((atoms, width), bf16),
            shape((cells, slots), f32),
            shape((2, cells, slots), f32),
        ),
        in_specs=[vmem()] * (8 + len(sums)),
        out_specs=(vmem(),) * 3,
        compiler_params=grant(8),
        cost_estimate=cost(3_000_000_000, 3_000_000),
    )(
        message,
        phases,
        slab[0],
        hidden,
        aggregate,
        update_in,
        update_out,
        energy_weight.reshape(1, width),
        *sums,
    )

    return (
        features_out.reshape(features.shape),
        energy.reshape(species.shape),
        forces.reshape(offsets.shape),
    )


def solution(mesh):
    in_specs = (
        P(("groups", "gz"), "xy", None, None),
        P(("groups", "gz"), "xy", None),
        P(("groups", "gz"), "xy", None),
        P(None, ("groups", "gz"), "xy", None),
        P(("groups", "gz"), "xy", None, None),
        P(("groups", "gz"), "xy", None),
        P(("groups", "gz"), "xy", None, None),
        P(),
        P(),
        P(),
        P(),
        P(),
        P(),
        P(),
    )
    out_specs = (
        P(("groups", "gz"), "xy", None, None),
        P(("groups", "gz"), "xy", None),
        P(None, ("groups", "gz"), "xy", None),
    )
    return jax.shard_map(shards, mesh=mesh, in_specs=in_specs, out_specs=out_specs, check_vma=False)
```
